32 devices in a mesh: groups: 2 (over y), space: 4 (over z), chan: 4 (over x, core).
Axes of the slice: x: 2, y: 2, z: 4, core: 2. Of those that a mesh axis runs over, the one named last changes fastest.
Arguments:
- image: bfloat16 [384, 64, 256], P('chan', ('groups', 'space')), parts along dimension 1, may hold values from -6 to 6
- dw_weight: bfloat16 [384, 49], P('chan'), may hold values from -0.875 to 0.875
- ln_gain: float32 [384], P('chan'), may hold values from 0.1 to 1.9
- ln_shift: float32 [384], P('chan'), may hold values from -3 to 3
- w_in: bfloat16 [384, 1536], P(None, 'chan'), may hold values from -0.3125 to 0.3125
- b_in: float32 [1536], P('chan'), may hold values from -3 to 3
- w_out: bfloat16 [1536, 384], P('chan'), may hold values from -0.15625 to 0.15625
- layer_scale: float32 [384], P('chan'), may hold values from 0.3 to 1
- cotangent: bfloat16 [384, 64, 256], P('chan', ('groups', 'space')), parts along dimension 1, may hold values from -6 to 6
Outputs:
- output: bfloat16 [384, 64, 256], P('chan', ('groups', 'space')), parts along dimension 1
- d_image: bfloat16 [384, 64, 256], P('chan', ('groups', 'space')), parts along dimension 1
- d_kernel: float32 [384, 98], P('chan', 'groups'), parts along dimension 1
- d_gain: float32 [768], P(('groups', 'chan')), parts along dimension 0
- d_shift: float32 [768], P(('groups', 'chan')), parts along dimension 0
- d_w_in: float32 [384, 3072], P('space', ('groups', 'chan')), parts along dimension 1
- d_b_in: float32 [3072], P(('groups', 'chan')), parts along dimension 0
- d_w_out: float32 [3072, 384], P(('groups', 'chan'), 'space'), parts along dimension 0
- d_scale: float32 [768], P(('groups', 'chan')), parts along dimension 0
The draws below stay inside these ranges and needn't reach their ends.
There are 2 independent parts, one for each index of `groups`. The reference program is written for one: setup_inputs(seed, part) draws one part's arguments, and reference() takes and returns one part's arrays. A program takes and returns all parts, laid end to end along the dimension named above; an argument that names none is the same for every part. Nothing has to cross between parts.
All inputs are finite; a program needn't handle non-finite values.
Results may differ from the reference program's by a relative error of at most 0.012.
Values may be sent and summed in bfloat16 or wider, within the bound.
No kernel may reach another device: no remote copies, remote signals or barrier semaphores. Data moves between devices by JAX's collectives and lax.ppermute only.
A program may use at most 64 MiB of HBM per device.

```python
import math
import jax
import jax.numpy as jnp
from jax import lax

D = 384
HID = 1536
TAPS = 49
COLS = 256
ROWS = 32
N_CHAN = 4


def level_of(key, extent, shards, low, top_value):
    def one(dim, blocks):
        heights = jax.random.uniform(jax.random.fold_in(jax.random.fold_in(key, 6), dim), (blocks,), jnp.float32, low / len(shards), top_value / len(shards))
        return jnp.repeat(jnp.exp(heights), extent[dim] // blocks).reshape((-1,) + (1,) * (len(extent) - dim - 1))

    level = one(*shards[0])
    for cut in shards[1:]:
        level = level * one(*cut)
    return level


def gaussian(key, shape, spread, limit, shards=(), dtype=jnp.bfloat16):
    values = spread * jax.random.normal(key, shape, jnp.float32)
    if shards:
        values = values * level_of(key, shape, shards, -0.22, 0.18)
    return jnp.clip(values, -limit, limit).astype(dtype)


def setup_inputs(seed: int = 0, part: int = 0) -> dict:
    splits = jax.random.split(jax.random.key(seed), 10)
    part_keys = jax.random.split(jax.random.fold_in(splits[9], part), 10)
    return {
        "image": gaussian(part_keys[0], (D, ROWS, COLS), 1.0, 6.0, ((0, 4), (1, 4))),
        "dw_weight": gaussian(splits[1], (D, TAPS), TAPS ** -0.5, 0.875, ((0, 4),)),
        "ln_gain": jnp.clip(1.0 + 0.18 * jax.random.normal(splits[2], (D,), jnp.float32), 0.1, 1.9),
        "ln_shift": gaussian(splits[3], (D,), 0.5, 3.0, ((0, 4),), jnp.float32),
        "w_in": gaussian(splits[4], (D, HID), D ** -0.5, 0.3125, ((1, 4),)),
        "b_in": gaussian(splits[5], (HID,), 0.5, 3.0, ((0, 4),), jnp.float32),
        "w_out": gaussian(splits[6], (HID, D), HID ** -0.5, 0.15625, ((0, 4),)),
        "layer_scale": jnp.clip(jnp.exp(math.log(1.0) - 1.2039728 * jax.random.uniform(splits[7], (D,), jnp.float32) ** level_of(splits[7], (D,), ((0, 4),), -0.2, 0.2)), 0.3, 1.0),
        "cotangent": gaussian(part_keys[8], (D, ROWS, COLS), 1.0, 6.0, ((0, 4), (1, 4))),
    }


grad_scale = 1.0 / 128.0

def depthwise(padded, kernel, height, width):
    total = jnp.zeros((padded.shape[0], height, width), jnp.float32)
    for row_tap in range(7):
        for col_tap in range(7):
            weight = kernel[:, row_tap * 7 + col_tap][:, None, None]
            total = total + weight * padded[:, row_tap:row_tap + height, col_tap:col_tap + width]
    return total

def flipped(padded, kernel, height, width):
    total = jnp.zeros((padded.shape[0], height, width), jnp.float32)
    for row_tap in range(7):
        for col_tap in range(7):
            weight = kernel[:, row_tap * 7 + col_tap][:, None, None]
            total = total + weight * padded[:, 6 - row_tap:6 - row_tap + height, 6 - col_tap:6 - col_tap + width]
    return total

def kernel_grad(grad, padded, height, width):
    columns = []
    for row_tap in range(7):
        for col_tap in range(7):
            window = padded[:, row_tap:row_tap + height, col_tap:col_tap + width]
            columns.append(lax.optimization_barrier(jnp.sum(grad * window, axis=(1, 2))))
    return jnp.stack(columns, axis=1)

def gelu_tanh(values):
    return jax.nn.gelu(values, approximate=True)

def blocked_sum(left, right, blocks, left_rows):
    size = right.shape[0] // blocks
    total = jnp.zeros((left.shape[1] if left_rows else left.shape[0], right.shape[1]), jnp.float32)
    for index in range(blocks):
        if left_rows:
            term = jnp.dot(left[index * size:(index + 1) * size].T, right[index * size:(index + 1) * size], preferred_element_type=jnp.float32)
        else:
            term = jnp.dot(left[:, index * size:(index + 1) * size], right[index * size:(index + 1) * size], preferred_element_type=jnp.float32)
        rounded = lax.optimization_barrier(term.astype(jnp.bfloat16))
        total = total + rounded.astype(jnp.float32)
    return total

def reference(image, dw_weight, ln_gain, ln_shift, w_in, b_in, w_out, layer_scale, cotangent):
    channels, height, width = image.shape
    source = image.astype(jnp.float32)
    kernel = dw_weight.astype(jnp.float32)
    padded = jnp.pad(source, ((0, 0), (3, 3), (3, 3)))
    conv = depthwise(padded, kernel, height, width).reshape(channels, height * width)
    average = lax.optimization_barrier(jnp.mean(conv, axis=0))
    centered = conv - average
    variance = lax.optimization_barrier(jnp.mean(centered * centered, axis=0))
    inv_std = lax.rsqrt(variance + 1e-06)
    standard = centered * inv_std
    normed = (standard * ln_gain[:, None] + ln_shift[:, None]).astype(jnp.bfloat16)
    pre = jnp.dot(w_in.T, normed, preferred_element_type=jnp.float32) + b_in[:, None]
    active = gelu_tanh(pre).astype(jnp.bfloat16)
    branch = blocked_sum(w_out, active, N_CHAN, True)
    output = (source + (layer_scale[:, None] * branch).reshape(channels, height, width)).astype(jnp.bfloat16)
    upstream = cotangent.astype(jnp.float32).reshape(channels, height * width)
    d_scale = lax.optimization_barrier(jnp.sum(upstream * branch, axis=1)) * grad_scale
    dbranch = (upstream * layer_scale[:, None]).astype(jnp.bfloat16)
    d_w_out = jnp.dot(active, dbranch.T, preferred_element_type=jnp.float32) * grad_scale
    dactive = jnp.dot(w_out, dbranch, preferred_element_type=jnp.float32)
    unused, pullback = jax.vjp(gelu_tanh, pre)
    dpre = pullback(dactive)[0]
    d_b_in = lax.optimization_barrier(jnp.sum(dpre, axis=1)) * grad_scale
    dpre_half = dpre.astype(jnp.bfloat16)
    d_w_in = jnp.dot(normed, dpre_half.T, preferred_element_type=jnp.float32) * grad_scale
    dnormed = blocked_sum(w_in, dpre_half, N_CHAN, False)
    d_shift = lax.optimization_barrier(jnp.sum(dnormed, axis=1)) * grad_scale
    d_gain = lax.optimization_barrier(jnp.sum(dnormed * standard, axis=1)) * grad_scale
    dstandard = dnormed * ln_gain[:, None]
    first = lax.optimization_barrier(jnp.mean(dstandard, axis=0))
    second = lax.optimization_barrier(jnp.mean(dstandard * standard, axis=0))
    dconv = (inv_std * (dstandard - first - standard * second)).astype(jnp.bfloat16)
    grad_field = dconv.astype(jnp.float32).reshape(channels, height, width)
    grad_pad = jnp.pad(grad_field, ((0, 0), (3, 3), (3, 3)))
    dsource = flipped(grad_pad, kernel, height, width)
    d_kernel = kernel_grad(grad_field, padded, height, width) * grad_scale
    d_image = (cotangent.astype(jnp.float32) + dsource).astype(jnp.bfloat16)
    return (output, d_image, d_kernel, d_gain, d_shift, d_w_in, d_b_in, d_w_out, d_scale)
```

```python
import functools

import jax
import jax.numpy as jnp
import numpy as np
from jax import lax
from jax.experimental import pallas as pl
from jax.experimental.pallas import tpu as pltpu
from jax.sharding import PartitionSpec as P

BF = jnp.bfloat16
F32 = jnp.float32
grad_scale = 1.0 / 128.0
SLOTS = 16
VMEM = pl.BlockSpec(memory_space=pltpu.VMEM)
SMEM = pl.BlockSpec(memory_space=pltpu.SMEM)
PARAMS = pltpu.CompilerParams(vmem_limit_bytes=40 << 20)
HI = lax.Precision.HIGHEST
NT = (((1,), (1,)), ((), ()))


def slot_row(slot, height):
    if slot < height:
        return slot
    if slot < height + 3:
        return slot - height - 3
    if slot < height + 6:
        return slot - 3
    return None


def tap_table(height, flip):
    table = np.zeros((height, 64, 8 * SLOTS), np.float32)
    for h in range(height):
        for s in range(7):
            for slot in range(SLOTS):
                row = slot_row(slot, height)
                if row is None:
                    continue
                r = h + 3 - row if flip else row - h + 3
                if 0 <= r < 7:
                    table[h, 7 * r + s, s * SLOTS + slot] = 1.0
    return table.astype(BF)


def shifted(tile, by):
    width = tile.shape[1]
    if by == 0:
        return tile
    lane = lax.broadcasted_iota(jnp.int32, tile.shape, 1)
    inside = lane < width - by if by > 0 else lane >= -by
    return jnp.where(inside, pltpu.roll(tile, (-by) % width, 1), 0.0)


def stack_shifts(tile, sign):
    parts = [shifted(tile, sign * (s - 3)).astype(BF) for s in range(7)]
    parts.append(jnp.zeros(tile.shape, BF))
    return jnp.concatenate(parts, axis=0)


def spread_taps(weight_ref, table_ref, taps_ref, height, local):
    for h in range(height):
        taps_ref[pl.ds(h * local, local), :] = jnp.dot(
            weight_ref[...], table_ref[h], preferred_element_type=F32
        )


def conv_kernel(core_ref, image_ref, halo_ref, weight_ref, table_ref, own_ref, send_ref, taps_ref, acc_ref):
    local, height, width = image_ref.shape
    spread_taps(weight_ref, table_ref, taps_ref, height, local)

    def body(i, carry):
        for u in range(8):
            ch = i * 8 + u
            tile = jnp.concatenate([image_ref[ch].astype(F32), halo_ref[ch].astype(F32)], axis=0)
            taps = taps_ref[pl.ds(ch, height, stride=local), :].astype(BF)
            value = jnp.dot(taps, stack_shifts(tile, 1), preferred_element_type=F32)
            for half in range(2):
                lanes = slice(half * 128, half * 128 + 128)
                acc_ref[half, pl.ds(ch, height, stride=local), :] = value[:, lanes]
        return carry

    lax.fori_loop(0, local // 8, body, 0)
    core = core_ref[0]
    rows = height // 2 * local
    for half in range(2):
        lanes = slice(half * 128, half * 128 + 128)
        mine = pl.multiple_of(core * rows, 16)
        theirs = pl.multiple_of((1 - core) * rows, 16)
        own_ref[:, lanes] = acc_ref[half, pl.ds(mine, rows), :].astype(BF)
        send_ref[:, lanes] = acc_ref[half, pl.ds(theirs, rows), :].astype(BF)


def conv_forward(core, image, halo, weight, table):
    local, height, width = image.shape
    rows = height // 2 * local
    return pl.pallas_call(
        conv_kernel,
        out_shape=[jax.ShapeDtypeStruct((rows, width), BF)] * 2,
        in_specs=[SMEM, VMEM, VMEM, VMEM, VMEM],
        out_specs=[VMEM, VMEM],
        scratch_shapes=[
            pltpu.VMEM((height * local, 8 * SLOTS), F32),
            pltpu.VMEM((2, height * local, 128), F32),
        ],
        compiler_params=PARAMS,
        name="conv_forward",
    )(core, image, halo, weight, table)


def mlp_kernel(blocks, me_ref, *refs):
    conv_refs = refs[:blocks]
    ct_refs = refs[blocks : 2 * blocks]
    (gain_ref, shift_ref, w_in_ref, w_inx_ref, w_int_ref, w_intx_ref, w_out_ref, w_outx_ref,
     w_outt_ref, w_outtx_ref, b_ref, bx_ref) = refs[2 * blocks : 2 * blocks + 12]
    (branch_ref, dn_ref, dn_own_ref, stand_ref, inv_ref, q_ref, own_ref, send_ref, db_ref,
     normed, centred, dbranch, acc_ref, bias_ref) = refs[2 * blocks + 12 :]
    step = pl.program_id(0)
    me = me_ref[0]
    local = conv_refs[0].shape[0]
    width = conv_refs[0].shape[1]
    channels = blocks * local
    hid = w_in_ref.shape[1]

    @pl.when(step == 0)
    def _():
        acc_ref[...] = jnp.zeros_like(acc_ref)
        bias_ref[...] = jnp.zeros_like(bias_ref)

    def where(j):
        return pl.ds(pl.multiple_of((me ^ j) * local, 16), local)

    total = jnp.zeros((1, width), F32)
    for j in range(blocks):
        value = conv_refs[j][...].astype(F32)
        centred[where(j), :] = value
        total = total + jnp.sum(value, axis=0, keepdims=True)
        dbranch[where(j), :] = ct_refs[j][...]
    average = total / channels
    value = centred[...] - average
    variance = jnp.sum(value * value, axis=0, keepdims=True) / channels
    inv_std = lax.rsqrt(variance + 1e-06)
    inv_ref[0] = inv_std
    for j in range(blocks):
        stand = (centred[where(j), :] - average) * inv_std
        rows = pl.ds(j * local, local)
        normed[where(j), :] = (stand * gain_ref[rows, :] + shift_ref[rows, :]).astype(BF)
        centred[where(j), :] = stand
    chip = pl.ds(pl.multiple_of((me // 2) * 2 * local, 16), 2 * local)
    stand_ref[...] = centred[chip, :]
    x = normed[...]
    d = dbranch[...]
    branch = jnp.zeros((channels, width), F32)
    dnormed = jnp.zeros((channels, width), F32)
    parts = ((w_in_ref, w_int_ref, w_out_ref, w_outt_ref, b_ref),
             (w_inx_ref, w_intx_ref, w_outx_ref, w_outtx_ref, bx_ref))
    k0, k1 = (0.7978845608028654, 0.044715)
    for part, (w_in, w_int, w_out, w_outt, bias) in enumerate(parts):
        pre = jnp.dot(w_int[...], x, preferred_element_type=F32) + bias[...]
        dact = jnp.dot(w_out[...], d, preferred_element_type=F32)
        square = pre * pre
        th = jnp.tanh(pre * (k0 + (k0 * k1) * square))
        half = 0.5 * pre
        active = (half + half * th).astype(BF)
        slope = 0.5 + 0.5 * th + half * (1.0 - th * th) * (k0 + (3.0 * k0 * k1) * square)
        dpre = dact * slope
        bias_ref[part] += dpre[:, :128] + dpre[:, 128:]
        dhalf = dpre.astype(BF)
        branch += jnp.dot(w_outt[...], active, preferred_element_type=F32)
        dnormed += jnp.dot(w_in[...], dhalf, preferred_element_type=F32)
        acc_ref[2 * part] += lax.dot_general(x, dhalf, NT, preferred_element_type=F32)
        acc_ref[2 * part + 1] += lax.dot_general(d, active, NT, preferred_element_type=F32)
    stand = centred[...]
    centred[...] = branch
    for j in range(blocks):
        branch_ref[j] = centred[where(j), :].astype(BF)
    centred[...] = dnormed
    first = jnp.zeros((1, width), F32)
    for k in range(blocks // 2):
        rows = pl.ds(pl.multiple_of(((me // 2) ^ k) * 2 * local, 16), 2 * local)
        if k == 0:
            dn_own_ref[...] = centred[rows, :]
        else:
            dn_ref[k - 1] = centred[rows, :].astype(BF)
    dbranch_gain = jnp.zeros((1, width), F32)
    for j in range(blocks):
        scaled = centred[where(j), :] * gain_ref[pl.ds(j * local, local), :]
        first = first + jnp.sum(scaled, axis=0, keepdims=True)
        centred[where(j), :] = scaled
    second = jnp.sum(centred[...] * stand, axis=0, keepdims=True)
    q_ref[0] = jnp.concatenate([first, second], axis=0)

    @pl.when(step == pl.num_programs(0) - 1)
    def _():
        for i in range(2):
            own_ref[i] = acc_ref[i]
            send_ref[i] = acc_ref[2 + i].astype(BF)
            db_ref[i] = lax.dot_general(
                jnp.ones((8, 128), F32), bias_ref[i], NT, preferred_element_type=F32, precision=HI
            )


def mlp(me, conv, ct, gain, shift, weights, biases):
    blocks = len(conv)
    rows, width = conv[0].shape
    local = gain.shape[0] // blocks
    steps = rows // local
    channels = blocks * local
    hid = weights[0].shape[1]
    tile = pl.BlockSpec((local, width), lambda i: (i, 0))

    def whole(a):
        return pl.BlockSpec(a.shape, lambda i: (0,) * a.ndim)

    small = [gain, shift, *weights, *biases]
    out_shape = [
        jax.ShapeDtypeStruct((blocks, rows, width), BF),
        jax.ShapeDtypeStruct((max(blocks // 2 - 1, 1), 2 * rows, width), BF),
        jax.ShapeDtypeStruct((2 * rows, width), F32),
        jax.ShapeDtypeStruct((2 * rows, width), F32),
        jax.ShapeDtypeStruct((steps, 1, width), F32),
        jax.ShapeDtypeStruct((steps, 2, width), F32),
        jax.ShapeDtypeStruct((2, channels, hid), F32),
        jax.ShapeDtypeStruct((2, channels, hid), BF),
        jax.ShapeDtypeStruct((2, 8, hid), F32),
    ]
    peers = out_shape[1].shape[0]
    out_specs = [
        pl.BlockSpec((blocks, local, width), lambda i: (0, i, 0)),
        pl.BlockSpec((peers, 2 * local, width), lambda i: (0, i, 0)),
        pl.BlockSpec((2 * local, width), lambda i: (i, 0)),
        pl.BlockSpec((2 * local, width), lambda i: (i, 0)),
        pl.BlockSpec((1, 1, width), lambda i: (i, 0, 0)),
        pl.BlockSpec((1, 2, width), lambda i: (i, 0, 0)),
        pl.BlockSpec((2, channels, hid), lambda i: (0, 0, 0)),
        pl.BlockSpec((2, channels, hid), lambda i: (0, 0, 0)),
        pl.BlockSpec((2, 8, hid), lambda i: (0, 0, 0)),
    ]
    return pl.pallas_call(
        functools.partial(mlp_kernel, blocks),
        grid=(steps,),
        out_shape=out_shape,
        in_specs=[SMEM] + [tile] * (2 * blocks) + [whole(a) for a in small],
        out_specs=out_specs,
        scratch_shapes=[
            pltpu.VMEM((channels, width), BF),
            pltpu.VMEM((channels, width), F32),
            pltpu.VMEM((channels, width), BF),
            pltpu.VMEM((4, channels, hid), F32),
            pltpu.VMEM((2, hid, 128), F32),
        ],
        compiler_params=PARAMS,
        name="mlp",
    )(me, *conv, *ct, *small)


def norm_kernel(peers, core_ref, *refs):
    dn_ref, stand_ref, inv_ref, gain_ref, q_ref = refs[:5]
    got = refs[5 : 5 + peers]
    got_q = refs[5 + peers : 5 + 2 * peers]
    (own_ref, send_ref, edge_own_ref, edge_send_ref, sums_ref, buf) = refs[5 + 2 * peers :]
    core = core_ref[0]
    steps = inv_ref.shape[0]
    both = dn_ref.shape[0] // steps
    local = both // 2
    channels = both * (peers + 1)
    shift_acc = jnp.zeros((both, 128), F32)
    gain_acc = jnp.zeros((both, 128), F32)
    for i in range(steps):
        rows = pl.ds(i * both, both)
        dn = dn_ref[rows, :]
        q = q_ref[i]
        for p in range(peers):
            dn = dn + got[p][0, rows, :].astype(F32)
            q = q + got_q[p][i]
        q = q / channels
        stand = stand_ref[rows, :]
        prod = dn * stand
        shift_acc += dn[:, :128] + dn[:, 128:]
        gain_acc += prod[:, :128] + prod[:, 128:]
        buf[i] = inv_ref[i] * (dn * gain_ref[...] - q[0:1] - stand * q[1:2])
    mine = pl.ds(pl.multiple_of(core * local, 16), local)
    theirs = pl.ds(pl.multiple_of((1 - core) * local, 16), local)
    for i in range(steps):
        own_ref[i] = buf[i, mine, :].astype(BF)
        send_ref[i] = buf[i, theirs, :].astype(BF)
    for i in range(3):
        edge_own_ref[i] = buf[i + core, mine, :].astype(BF)
        edge_send_ref[i] = buf[i + core, theirs, :].astype(BF)
    ones = jnp.ones((8, 128), F32)
    sums_ref[0] = lax.dot_general(ones, shift_acc, NT, preferred_element_type=F32, precision=HI)
    sums_ref[1] = lax.dot_general(ones, gain_acc, NT, preferred_element_type=F32, precision=HI)


def norm_backward(core, dn, stand, inv, gain, q, got, got_q):
    steps, _, width = inv.shape
    both = dn.shape[0] // steps
    local = both // 2
    return pl.pallas_call(
        functools.partial(norm_kernel, len(got)),
        out_shape=[
            jax.ShapeDtypeStruct((steps, local, width), BF),
            jax.ShapeDtypeStruct((steps, local, width), BF),
            jax.ShapeDtypeStruct((3, local, width), BF),
            jax.ShapeDtypeStruct((3, local, width), BF),
            jax.ShapeDtypeStruct((2, 8, both), F32),
        ],
        in_specs=[SMEM] + [VMEM] * (5 + 2 * len(got)),
        out_specs=[VMEM] * 5,
        scratch_shapes=[pltpu.VMEM((steps, both, width), F32)],
        compiler_params=PARAMS,
        name="norm_backward",
    )(core, dn, stand, inv, gain, q, *got, *got_q)


def back_kernel(group, core_ref, own_ref, other_ref, same_ref, cross_ref, image_ref, ct_ref, weight_ref,
                table_ref, dimage_ref, dkernel_ref, taps_ref, rows_ref, corr_ref):
    local, height, width = image_ref.shape
    core = core_ref[0]
    spread_taps(weight_ref, table_ref, taps_ref, height, local)
    half = height // 2
    for part in range(2):
        lanes = slice(part * 128, part * 128 + 128)
        for i in range(half):
            rows_ref[part, pl.ds(pl.multiple_of((core * half + i) * local, 8), local), :] = (
                own_ref[i, :, lanes].astype(F32))
            rows_ref[part, pl.ds(pl.multiple_of(((1 - core) * half + i) * local, 8), local), :] = (
                other_ref[i, :, lanes].astype(F32))
        for i in range(3):
            a = pl.multiple_of((height + 3 * (1 - core) + i) * local, 8)
            b = pl.multiple_of((height + 3 * core + i) * local, 8)
            rows_ref[part, pl.ds(a, local), :] = same_ref[i, :, lanes].astype(F32)
            rows_ref[part, pl.ds(b, local), :] = cross_ref[i, :, lanes].astype(F32)
        rows_ref[part, pl.ds((height + 6) * local, 2 * local), :] = jnp.zeros((2 * local, 128), F32)

    span = group * height
    lane = lax.broadcasted_iota(jnp.int32, (8 * SLOTS, span), 1)
    slot = lax.broadcasted_iota(jnp.int32, (SLOTS, span), 0)
    lane_row = lax.broadcasted_iota(jnp.int32, (SLOTS, span), 1) % height
    row = jnp.where(slot < height, slot, jnp.where(slot < height + 3, slot - height - 3, slot - 3))
    row = jnp.where(slot < height + 6, row, 1000)
    pick = (lax.broadcasted_iota(jnp.int32, (group, span), 0)
            == lax.broadcasted_iota(jnp.int32, (group, span), 1) // height).astype(F32)

    for g in range(local // group):
        right = image_ref[pl.ds(g * group, group)].astype(F32).reshape(span, width).astype(BF)
        corr_ref[...] = jnp.zeros_like(corr_ref)

        def body(i, carry):
            for u in range(8):
                inner = i * 8 + u
                ch = g * group + inner
                tile = jnp.concatenate(
                    [rows_ref[p, pl.ds(ch, SLOTS, stride=local), :] for p in range(2)], axis=1)
                stack = stack_shifts(tile, -1)
                taps = taps_ref[pl.ds(ch, height, stride=local), :].astype(BF)
                value = jnp.dot(taps, stack, preferred_element_type=F32)
                dimage_ref[ch] = (ct_ref[ch].astype(F32) + value).astype(BF)
                corr = lax.dot_general(stack, right, NT, preferred_element_type=F32)
                corr_ref[...] = jnp.where(lane // height == inner, corr, corr_ref[...])
            return carry

        lax.fori_loop(0, group // 8, body, 0)
        lines = []
        for r in range(7):
            mask = row == lane_row - r + 3
            for s in range(7):
                block = corr_ref[pl.ds(s * SLOTS, SLOTS), :]
                lines.append(jnp.sum(jnp.where(mask, block, 0.0), axis=0, keepdims=True))
        lines.append(jnp.zeros((7, span), F32))
        dkernel_ref[pl.ds(g * group, group), :] = lax.dot_general(
            pick, jnp.concatenate(lines, axis=0), NT, preferred_element_type=F32, precision=HI)


def conv_backward(core, own, other, same, cross, image, ct, weight, table):
    local, height, width = image.shape
    group = 32 if local % 32 == 0 else 16
    return pl.pallas_call(
        functools.partial(back_kernel, group),
        out_shape=[
            jax.ShapeDtypeStruct((local, height, width), BF),
            jax.ShapeDtypeStruct((local, 56), F32),
        ],
        in_specs=[SMEM] + [VMEM] * 8,
        out_specs=[VMEM, VMEM],
        scratch_shapes=[
            pltpu.VMEM((height * local, 8 * SLOTS), F32),
            pltpu.VMEM((2, SLOTS * local, 128), F32),
            pltpu.VMEM((8 * SLOTS, group * height), F32),
        ],
        compiler_params=PARAMS,
        name="conv_backward",
    )(core, own, other, same, cross, image, ct, weight, table)


def swap(value, axis, size, k):
    return lax.ppermute(value, axis, [(i, i ^ k) for i in range(size)])


def sum_over_space(value, size):
    if size > 4:
        return lax.psum(value, "space")
    total = value
    for k in range(1, size):
        total = total + swap(value, "space", size, k)
    return total


def scatter_over_space(value, size):
    me = lax.axis_index("space")
    rows = value.shape[1] // size
    half = value.astype(BF)
    if size > 4:
        return lax.psum_scatter(half, "space", scatter_dimension=1, tiled=True).astype(F32)
    total = lax.dynamic_slice_in_dim(value, me * rows, rows, axis=1)
    for k in range(1, size):
        piece = lax.dynamic_slice_in_dim(half, (me ^ k) * rows, rows, axis=1)
        total = total + swap(piece, "space", size, k).astype(F32)
    return total


def per_device(image, dw_weight, ln_gain, ln_shift, w_in, b_in, w_out, layer_scale, cotangent):
    local, height, width = image.shape
    hid = w_in.shape[1]
    n_chan, n_space = lax.axis_size("chan"), lax.axis_size("space")
    half = height // 2
    me = lax.axis_index("chan")
    core = me % 2
    me_s, core_s = (me.astype(jnp.int32).reshape(1), core.astype(jnp.int32).reshape(1))
    up = [(i, i + 1) for i in range(n_space - 1)]
    down = [(i + 1, i) for i in range(n_space - 1)]

    before = lax.ppermute(image[:, height - 3 :], "space", up)
    after = lax.ppermute(image[:, :3], "space", down)
    weight = jnp.pad(dw_weight, ((0, 0), (0, 15)))
    packed = jnp.concatenate([ln_gain, ln_shift, b_in])
    vectors = [packed] + [swap(packed, "chan", n_chan, k) for k in range(1, n_chan)]
    gain = jnp.concatenate([v[:local] for v in vectors])[:, None]
    shift = jnp.concatenate([v[local : 2 * local] for v in vectors])[:, None]
    biases = [vectors[k][2 * local :][:, None] for k in range(2)]
    w_inx = swap(w_in, "chan", n_chan, 1)
    w_outx = swap(w_out, "chan", n_chan, 1)
    weights = [w_in, w_inx, w_in.T, w_inx.T, w_out, w_outx, w_out.T, w_outx.T]

    upstream = cotangent.astype(F32)
    dbranch = (upstream * layer_scale[:, None, None]).astype(BF).transpose(1, 0, 2)
    dbranch = dbranch.reshape(2, half * local, width)
    d_mine = lax.dynamic_index_in_dim(dbranch, core, 0, keepdims=False)
    d_theirs = lax.dynamic_index_in_dim(dbranch, 1 - core, 0, keepdims=False)
    d_all = [d_mine] + [
        swap(d_theirs if k % 2 else d_mine, "chan", n_chan, k) for k in range(1, n_chan)
    ]

    halo = jnp.concatenate([before, after, jnp.zeros((local, 2, width), BF)], axis=1)
    mine, theirs = conv_forward(core_s, image, halo, weight, tap_table(height, False))
    conv = [mine] + [swap(theirs if k % 2 else mine, "chan", n_chan, k) for k in range(1, n_chan)]
    (branch, dn_send, dn, stand, inv, q, dw_own, dw_send, d_b) = mlp(
        me_s, conv, d_all, gain, shift, weights, biases)

    got_q = [swap(q, "chan", n_chan, 2 * k) for k in range(1, n_chan // 2)]
    got = [swap(dn_send[k - 1 : k], "chan", n_chan, 2 * k) for k in range(1, n_chan // 2)]
    dw = dw_own + swap(dw_send, "chan", n_chan, 1).astype(F32)
    dw = scatter_over_space(dw, n_space)

    g_own = gain[:local]
    g_other = gain[local : 2 * local]
    g_pair = jnp.where(core == 0, jnp.concatenate([g_own, g_other]), jnp.concatenate([g_other, g_own]))
    dconv, dconv_send, edge, edge_send, sums = norm_backward(core_s, dn, stand, inv, g_pair, q, got, got_q)
    other = swap(dconv_send, "chan", n_chan, 1)
    same_pairs, cross_pairs = [], []
    for s in range(n_space):
        for c in range(n_chan):
            t = s + 1 if c % 2 else s - 1
            if 0 <= t < n_space:
                same_pairs.append((s * n_chan + c, t * n_chan + c))
                cross_pairs.append((s * n_chan + c, t * n_chan + (c ^ 1)))
    same = lax.ppermute(edge, ("space", "chan"), same_pairs)
    cross = lax.ppermute(edge_send, ("space", "chan"), cross_pairs)

    parts = [branch[0]] + [swap(branch[k], "chan", n_chan, k) for k in range(1, n_chan)]
    b_mine = sum(p.astype(F32) for p in parts[0::2])
    b_theirs = sum(p.astype(F32) for p in parts[1::2])
    total = jnp.where(core == 0, jnp.stack([b_mine, b_theirs]), jnp.stack([b_theirs, b_mine]))
    total = total.reshape(height, local, width).transpose(1, 0, 2)
    output = (image.astype(F32) + layer_scale[:, None, None] * total).astype(BF)
    d_scale = jnp.sum(upstream * total, axis=(1, 2))

    d_image, d_kernel = conv_backward(
        core_s, dconv, other, same, cross, image, cotangent, weight, tap_table(height, True))

    sums = sums[:, 0].reshape(2, 2, local)
    s_mine = lax.dynamic_index_in_dim(sums, core, 1, keepdims=False)
    s_theirs = lax.dynamic_index_in_dim(sums, 1 - core, 1, keepdims=False)
    cross_core = swap(jnp.concatenate([s_theirs.reshape(-1), d_b[1, 0]]), "chan", n_chan, 1)
    vector = jnp.concatenate([s_mine.reshape(-1), d_b[0, 0]]) + cross_core
    vector = jnp.concatenate([vector, d_scale, d_kernel[:, :49].reshape(-1)])
    vector = sum_over_space(vector, n_space) * grad_scale
    d_shift, d_gain = vector[:local], vector[local : 2 * local]
    d_b_in = vector[2 * local : 2 * local + hid]
    d_scale = vector[2 * local + hid : 3 * local + hid]
    d_kernel = vector[3 * local + hid :].reshape(local, 49)
    dw = dw * grad_scale
    return (output, d_image, d_kernel, d_gain, d_shift, dw[0], d_b_in, dw[1].T, d_scale)


def solution(mesh):
    return jax.shard_map(
        per_device,
        mesh=mesh,
        in_specs=(
            P("chan", ("groups", "space"), None),
            P("chan", None),
            P("chan"),
            P("chan"),
            P(None, "chan"),
            P("chan"),
            P("chan", None),
            P("chan"),
            P("chan", ("groups", "space"), None),
        ),
        out_specs=(
            P("chan", ("groups", "space"), None),
            P("chan", ("groups", "space"), None),
            P("chan", "groups"),
            P(("groups", "chan")),
            P(("groups", "chan")),
            P("space", ("groups", "chan")),
            P(("groups", "chan")),
            P(("groups", "chan"), "space"),
            P(("groups", "chan")),
        ),
        check_vma=False,
    )
```

```python
import functools

import jax
import jax.numpy as jnp
from jax import lax
from jax.experimental import pallas as pl
from jax.experimental.pallas import tpu as pltpu
from jax.sharding import PartitionSpec as P

BF = jnp.bfloat16
F32 = jnp.float32
grad_scale = 1.0 / 128.0
SLOTS = 16
VMEM = pl.BlockSpec(memory_space=pltpu.VMEM)
SMEM = pl.BlockSpec(memory_space=pltpu.SMEM)


def cost(microseconds):
    return pl.CostEstimate(flops=int(microseconds * 1.1e9), bytes_accessed=0, transcendentals=0)


def grant(mib):
    return pltpu.CompilerParams(vmem_limit_bytes=mib << 20)


HI = lax.Precision.HIGHEST
NT = (((1,), (1,)), ((), ()))


def column(row):
    return jnp.broadcast_to(row, (8, row.shape[1])).T[:, :1]


def shift_halves(a, b, by):
    if by == 0:
        return a, b
    lane = lax.broadcasted_iota(jnp.int32, a.shape, 1)
    k = (-by) % 128
    ra, rb = pltpu.roll(a, k, 1), pltpu.roll(b, k, 1)
    if by > 0:
        inner = lane < 128 - by
        return jnp.where(inner, ra, rb), jnp.where(inner, rb, 0.0)
    inner = lane >= -by
    return jnp.where(inner, ra, 0.0), jnp.where(inner, rb, ra)


def taps_kernel(flip, height, weight_ref, out_ref, rows_ref):
    local = out_ref.shape[0] // (7 * height)
    count = 7 * height
    tap = lax.broadcasted_iota(jnp.int32, (64, 128), 0)
    slot = lax.broadcasted_iota(jnp.int32, (64, 128), 1) % SLOTS
    row = jnp.where(slot < height + 3, slot, slot - SLOTS)
    weight = weight_ref[...].astype(F32).T[:local].astype(BF)
    for h in range(height):
        r = h + 3 - row if flip else row - h + 3
        base = jnp.where((r >= 0) & (r < 7) & (row >= -3), 7 * r, -100)
        for s in range(7):
            table = (tap == base + s).astype(F32).astype(BF)
            rows_ref[pl.ds((s * height + h) * local, local), :] = jnp.dot(
                weight, table, preferred_element_type=F32)
    lane = lax.broadcasted_iota(jnp.int32, (count, 128), 1) // SLOTS

    def body(g, carry):
        for u in range(0, 8, 2):
            pair = [
                jnp.where(lane == u + v, rows_ref[pl.ds(g * 8 + u + v, count, stride=local), :], 0.0)
                for v in range(2)
            ]
            start = pl.multiple_of((g * 8 + u) * count, 16)
            out_ref[pl.ds(start, 2 * count), :] = jnp.concatenate(pair, axis=0).astype(BF)
        return carry

    lax.fori_loop(0, local // 8, body, 0)


def make_taps(weight, local, height, flip):
    count = 7 * height
    return pl.pallas_call(
        functools.partial(taps_kernel, flip, height),
        out_shape=jax.ShapeDtypeStruct((local * count, 128), BF),
        in_specs=[VMEM],
        out_specs=VMEM,
        scratch_shapes=[pltpu.VMEM((count * local, 128), F32)],
        compiler_params=grant(6),
        cost_estimate=cost(2.4),
        name="taps_back" if flip else "taps_forward",
    )(weight)


def vector_of(lines, count):
    lines = lines.astype(F32)
    return [
        lines[r : r + 1] + lines[count + r : count + r + 1] + lines[2 * count + r : 2 * count + r + 1]
        for r in range(count)
    ]


def edge_kernel(ids_ref, image_ref, edge_a_ref, edge_b_ref, rows_ref):
    local, height, width = image_ref.shape
    odd = ids_ref[1] & 1

    def body(g, carry):
        for u in range(8):
            tile = image_ref[g * 8 + u].astype(F32)
            for part in range(2):
                rows_ref[part, pl.ds(g * 8 + u, height, stride=local), :] = tile[:, part * 128 : part * 128 + 128]
        return carry

    lax.fori_loop(0, local // 8, body, 0)
    top, bottom = (0, (height - 3) * local)
    for part in range(2):
        lanes = slice(part * 128, part * 128 + 128)
        to_a = pl.multiple_of(jnp.where(odd == 0, bottom, top), 16)
        to_b = pl.multiple_of(jnp.where(odd == 0, top, bottom), 16)
        edge_a_ref[:, lanes] = rows_ref[part, pl.ds(to_a, 3 * local), :].astype(BF)
        edge_b_ref[:, lanes] = rows_ref[part, pl.ds(to_b, 3 * local), :].astype(BF)


def edges(ids, image):
    local, height, width = image.shape
    return pl.pallas_call(
        edge_kernel,
        out_shape=[jax.ShapeDtypeStruct((3 * local, width), BF)] * 2,
        in_specs=[SMEM, VMEM],
        out_specs=[VMEM, VMEM],
        scratch_shapes=[pltpu.VMEM((2, height * local, 128), F32)],
        compiler_params=grant(3),
        cost_estimate=cost(1.2),
        name="edges",
    )(ids, image)


def pack_kernel(ids_ref, ct_ref, vector_ref, own_ref, send_ref, rows_ref, col_ref):
    local, height, width = ct_ref.shape
    core = ids_ref[0] & 1
    vector = vector_ref[...]
    count = vector.shape[1] // width
    col_ref[...] = column(vector)
    scale = col_ref[pl.ds(vector.shape[1] - 128, local), :]
    high = vector.astype(BF).astype(F32)
    middle = (vector - high).astype(BF).astype(F32)
    low = vector - high - middle
    lines = [part[:, r * width : r * width + width] for part in (high, middle, low) for r in range(count)]
    lines = jnp.concatenate(lines + [jnp.zeros((16 - 3 * count, width), F32)], axis=0).astype(BF)
    own_ref[pl.ds(height // 2 * local, 16), :] = lines
    send_ref[pl.ds(height // 2 * local, 16), :] = lines

    def body(g, carry):
        for u in range(8):
            tile = ct_ref[g * 8 + u].astype(F32)
            for part in range(2):
                rows_ref[part, pl.ds(g * 8 + u, height, stride=local), :] = tile[:, part * 128 : part * 128 + 128]
        return carry

    lax.fori_loop(0, local // 8, body, 0)
    for i in range(height // 2):
        rows = pl.ds(i * local, local)
        mine = pl.multiple_of((core * (height // 2) + i) * local, 16)
        theirs = pl.multiple_of(((1 - core) * (height // 2) + i) * local, 16)
        for part in range(2):
            lanes = slice(part * 128, part * 128 + 128)
            own_ref[rows, lanes] = (rows_ref[part, pl.ds(mine, local), :] * scale).astype(BF)
            send_ref[rows, lanes] = (rows_ref[part, pl.ds(theirs, local), :] * scale).astype(BF)


def pack(ids, ct, vector):
    local, height, width = ct.shape
    return pl.pallas_call(
        pack_kernel,
        out_shape=[jax.ShapeDtypeStruct((height // 2 * local + 16, width), BF)] * 2,
        in_specs=[SMEM, VMEM, VMEM],
        out_specs=[VMEM, VMEM],
        scratch_shapes=[
            pltpu.VMEM((2, height * local, 128), F32),
            pltpu.VMEM((vector.shape[1], 1), F32),
        ],
        compiler_params=grant(4),
        cost_estimate=cost(1.4),
        name="pack",
    )(ids, ct, vector)


def turn_kernel(*refs):
    for source, out in zip(refs[:4], refs[4:]):
        out[...] = source[...].T


def turn(*weights):
    return pl.pallas_call(
        turn_kernel,
        out_shape=[jax.ShapeDtypeStruct(w.shape[::-1], BF) for w in weights],
        in_specs=[VMEM] * 4,
        out_specs=[VMEM] * 4,
        compiler_params=grant(5),
        cost_estimate=cost(0.4),
        name="turn",
    )(*weights)


def merge_kernel(ids_ref, own_ref, got_ref, mine_ref, *rest):
    outs, buf = rest[:-1], rest[-1]
    rows = mine_ref.shape[1]
    me = ids_ref[1]
    for p in range(2):
        buf[...] = own_ref[p].astype(F32) + got_ref[p].astype(F32)
        mine_ref[p] = buf[pl.ds(pl.multiple_of(me * rows, 8), rows), :]
        for k, out in enumerate(outs):
            out[p] = buf[pl.ds(pl.multiple_of((me ^ (k + 1)) * rows, 8), rows), :].astype(BF)


def merge(ids, own, got, size):
    rows, hid = own.shape[1] // size, own.shape[2]
    return pl.pallas_call(
        merge_kernel,
        out_shape=[jax.ShapeDtypeStruct((2, rows, hid), F32)]
        + [jax.ShapeDtypeStruct((2, rows, hid), BF)] * (size - 1),
        in_specs=[SMEM, VMEM, VMEM],
        out_specs=[VMEM] * size,
        scratch_shapes=[pltpu.VMEM(own.shape[1:], F32)],
        compiler_params=grant(5),
        cost_estimate=cost(1),
        name="merge",
    )(ids, own, got)


def shift_sum(products, height, sign):
    left = products[3 * height : 4 * height, :128]
    right = products[3 * height : 4 * height, 128:]
    for s in (0, 1, 2, 4, 5, 6):
        block = products[s * height : (s + 1) * height]
        a, b = shift_halves(block[:, :128], block[:, 128:], sign * (s - 3))
        left, right = left + a, right + b
    return left, right


def conv_kernel(ids_ref, image_ref, got_a_ref, got_b_ref, taps_ref, own_ref, send_ref, image16_ref, acc_ref, rim_ref):
    local, height, width = image_ref.shape
    rows = own_ref.shape[0]
    count = 7 * height
    core, odd = ids_ref[0] & 1, ids_ref[1] & 1
    for part in range(2):
        lanes = slice(part * 128, part * 128 + 128)
        to_a = pl.multiple_of(5 * odd * local, 16)
        to_b = pl.multiple_of(5 * (1 - odd) * local, 16)
        rim_ref[part, pl.ds(to_a, 3 * local), :] = got_a_ref[:, lanes].astype(F32)
        rim_ref[part, pl.ds(to_b, 3 * local), :] = got_b_ref[:, lanes].astype(F32)
        rim_ref[part, pl.ds(3 * local, 2 * local), :] = jnp.zeros((2 * local, 128), F32)

    def body(g, carry):
        for u in range(8):
            ch = g * 8 + u
            pair = [rim_ref[p, pl.ds(ch, SLOTS - height, stride=local), :] for p in range(2)]
            tile = jnp.concatenate([image_ref[ch].astype(F32), jnp.concatenate(pair, axis=1)], axis=0)
            image16_ref[ch] = tile.astype(BF)
        right = image16_ref[pl.ds(g * 8, 8)].reshape(8 * SLOTS, width)
        taps = taps_ref[pl.ds(pl.multiple_of(g * 8 * count, 16), 8 * count), :]
        products = jnp.dot(taps, right, preferred_element_type=F32)
        for u in range(8):
            pair = shift_sum(products[u * count : (u + 1) * count], height, 1)
            for half in range(2):
                acc_ref[half, pl.ds(g * 8 + u, height, stride=local), :] = pair[half]
        return carry

    lax.fori_loop(0, local // 8, body, 0)
    for half in range(2):
        lanes = slice(half * 128, half * 128 + 128)
        mine = pl.multiple_of(core * rows, 16)
        theirs = pl.multiple_of((1 - core) * rows, 16)
        own_ref[:, lanes] = acc_ref[half, pl.ds(mine, rows), :].astype(BF)
        send_ref[:, lanes] = acc_ref[half, pl.ds(theirs, rows), :].astype(BF)


def conv_forward(ids, image, got_a, got_b, taps):
    local, height, width = image.shape
    rows = height // 2 * local
    return pl.pallas_call(
        conv_kernel,
        out_shape=[jax.ShapeDtypeStruct((rows, width), BF)] * 2
        + [jax.ShapeDtypeStruct((local, SLOTS, width), BF)],
        in_specs=[SMEM] + [VMEM] * 4,
        out_specs=[VMEM] * 3,
        scratch_shapes=[
            pltpu.VMEM((2, height * local, 128), F32),
            pltpu.VMEM((2, (SLOTS - height) * local, 128), F32),
        ],
        compiler_params=grant(6),
        cost_estimate=cost(5),
        name="conv_forward",
    )(ids, image, got_a, got_b, taps)


def mlp_kernel(blocks, me_ref, *refs):
    conv_refs = refs[:blocks]
    ct_refs = refs[blocks : 2 * blocks]
    vec_refs = refs[2 * blocks : 3 * blocks]
    (w_in_ref, w_inx_ref, w_int_ref, w_intx_ref, w_out_ref, w_outx_ref,
     w_outt_ref, w_outtx_ref) = refs[3 * blocks : 3 * blocks + 8]
    (branch_ref, dn_ref, dn_own_ref, stand_ref, inv_ref, q_ref, dw_ref, dwx_ref, small_ref, normed, centred, dbranch, acc_ref, bias_ref, col_ref) = refs[3 * blocks + 8 :]
    step = pl.program_id(0)
    me = me_ref[0]
    local = conv_refs[0].shape[0]
    width = conv_refs[0].shape[1]
    channels = blocks * local
    hid = w_in_ref.shape[1]

    @pl.when(step == 0)
    def _():
        acc_ref[...] = jnp.zeros_like(acc_ref)
        bias_ref[...] = jnp.zeros_like(bias_ref)
        for j in range(blocks):
            for r, line in enumerate(vector_of(vec_refs[j][...], col_ref.shape[1] // width)):
                col_ref[j, pl.ds(r * width, width), :] = column(line)

    def where(j):
        return pl.ds(pl.multiple_of((me ^ j) * local, 16), local)

    total = jnp.zeros((1, width), F32)
    for j in range(blocks):
        value = conv_refs[j][...].astype(F32)
        centred[where(j), :] = value
        total = total + jnp.sum(value, axis=0, keepdims=True)
        dbranch[where(j), :] = ct_refs[j][...]
    average = total / channels
    value = centred[...] - average
    variance = jnp.sum(value * value, axis=0, keepdims=True) / channels
    inv_std = lax.rsqrt(variance + 1e-06)
    inv_ref[0] = inv_std
    for j in range(blocks):
        stand = (centred[where(j), :] - average) * inv_std
        gain, shift = col_ref[j, pl.ds(0, local), :], col_ref[j, pl.ds(local, local), :]
        normed[where(j), :] = (stand * gain + shift).astype(BF)
        centred[where(j), :] = stand
    chip = pl.ds(pl.multiple_of((me // 2) * 2 * local, 16), 2 * local)
    stand_ref[...] = centred[chip, :]
    x = normed[...]
    d = dbranch[...]
    branch = jnp.zeros((channels, width), F32)
    dnormed = jnp.zeros((channels, width), F32)
    parts = ((w_in_ref, w_int_ref, w_out_ref, w_outt_ref),
             (w_inx_ref, w_intx_ref, w_outx_ref, w_outtx_ref))
    k0, k1 = (0.7978845608028654, 0.044715)
    for part, (w_in, w_int, w_out, w_outt) in enumerate(parts):
        bias = col_ref[part, pl.ds(2 * local, hid), :]
        pre = jnp.dot(w_int[...], x, preferred_element_type=F32) + bias
        dact = jnp.dot(w_out[...], d, preferred_element_type=F32)
        square = pre * pre
        th = jnp.tanh(pre * (k0 + (k0 * k1) * square))
        half = 0.5 * pre
        active = (half + half * th).astype(BF)
        slope = 0.5 + 0.5 * th + half * (1.0 - th * th) * (k0 + (3.0 * k0 * k1) * square)
        dpre = dact * slope
        bias_ref[part] += dpre[:, :128] + dpre[:, 128:]
        dhalf = dpre.astype(BF)
        branch += jnp.dot(w_outt[...], active, preferred_element_type=F32)
        dnormed += jnp.dot(w_in[...], dhalf, preferred_element_type=F32)
        acc_ref[2 * part] += lax.dot_general(x, dhalf, NT, preferred_element_type=F32)
        acc_ref[2 * part + 1] += lax.dot_general(d, active, NT, preferred_element_type=F32)
    stand = centred[...]
    centred[...] = branch
    for j in range(blocks):
        branch_ref[j] = centred[where(j), :].astype(BF)
    centred[...] = dnormed
    first = jnp.zeros((1, width), F32)
    for k in range(blocks // 2):
        rows = pl.ds(pl.multiple_of(((me // 2) ^ k) * 2 * local, 16), 2 * local)
        if k == 0:
            dn_own_ref[...] = centred[rows, :]
        else:
            dn_ref[k - 1, pl.ds(0, 2 * local), :] = centred[rows, :].astype(BF)
    for j in range(blocks):
        scaled = centred[where(j), :] * col_ref[j, pl.ds(0, local), :]
        first = first + jnp.sum(scaled, axis=0, keepdims=True)
        centred[where(j), :] = scaled
    second = jnp.sum(centred[...] * stand, axis=0, keepdims=True)
    q = jnp.concatenate([first, second], axis=0)
    q_ref[0] = q
    high = q.astype(BF)
    low = (q - high.astype(F32)).astype(BF)
    pad = jnp.zeros((12, width), F32)
    extra = jnp.concatenate([high.astype(F32), low.astype(F32), pad], axis=0).astype(BF)
    for k in range(1, blocks // 2):
        dn_ref[k - 1, pl.ds(2 * local, 16), :] = extra

    @pl.when(step == pl.num_programs(0) - 1)
    def _():
        ones = jnp.ones((8, 128), F32)
        for k in range(2):
            dw_ref[k] = acc_ref[k].astype(BF)
            dwx_ref[k] = acc_ref[2 + k].astype(BF)
        for j in range(blocks):
            prod = acc_ref[1, where(j), :] * w_outt_ref[where(j), :].astype(F32)
            prod = prod + acc_ref[3, where(j), :] * w_outtx_ref[where(j), :].astype(F32)
            if hid % 128:
                fold = jnp.pad(jnp.sum(prod, axis=1, keepdims=True), ((0, 0), (0, 127)))
            else:
                fold = sum(prod[:, i : i + 128] for i in range(128, hid, 128)) + prod[:, :128]
            sources = [fold] + [bias_ref[j, pl.ds(r * local, local), :] for r in range(hid // local if j < 2 else 0)]
            lines = [
                lax.dot_general(ones, a, NT, preferred_element_type=F32, precision=HI)[:1] for a in sources
            ]
            lines.append(jnp.zeros((8 - len(lines), local), F32))
            small_ref[j] = jnp.concatenate(lines, axis=0)


def mlp(me, conv, ct, lines, weights):
    blocks = len(conv)
    rows, width = conv[0].shape
    channels, hid = weights[0].shape
    local = channels // blocks
    steps = rows // local
    tile = pl.BlockSpec((local, width), lambda i: (i, 0))

    def whole(a):
        return pl.BlockSpec(a.shape, lambda i: (0,) * a.ndim)

    small = [*weights]
    last = pl.BlockSpec((16, width), lambda i: (rows // 16, 0))
    peers = max(blocks // 2 - 1, 1)
    out_shape = [
        jax.ShapeDtypeStruct((blocks, rows, width), BF),
        jax.ShapeDtypeStruct((peers, steps * (2 * local + 16), width), BF),
        jax.ShapeDtypeStruct((2 * rows, width), F32),
        jax.ShapeDtypeStruct((2 * rows, width), F32),
        jax.ShapeDtypeStruct((steps, 1, width), F32),
        jax.ShapeDtypeStruct((steps, 2, width), F32),
        *[jax.ShapeDtypeStruct((2, channels, hid), BF)] * 2,
        jax.ShapeDtypeStruct((blocks, 8, local), F32),
    ]
    out_specs = [
        pl.BlockSpec((blocks, local, width), lambda i: (0, i, 0)),
        pl.BlockSpec((peers, 2 * local + 16, width), lambda i: (0, i, 0)),
        pl.BlockSpec((2 * local, width), lambda i: (i, 0)),
        pl.BlockSpec((2 * local, width), lambda i: (i, 0)),
        pl.BlockSpec((1, 1, width), lambda i: (i, 0, 0)),
        pl.BlockSpec((1, 2, width), lambda i: (i, 0, 0)),
        *[pl.BlockSpec((2, channels, hid), lambda i: (0, 0, 0))] * 2,
        pl.BlockSpec((blocks, 8, local), lambda i: (0, 0, 0)),
    ]
    return pl.pallas_call(
        functools.partial(mlp_kernel, blocks),
        grid=(steps,),
        out_shape=out_shape,
        in_specs=[SMEM] + [tile] * (2 * blocks) + [last] * blocks + [whole(a) for a in small],
        out_specs=out_specs,
        scratch_shapes=[
            pltpu.VMEM((channels, width), BF),
            pltpu.VMEM((channels, width), F32),
            pltpu.VMEM((channels, width), BF),
            pltpu.VMEM((4, channels, hid), F32),
            pltpu.VMEM((2, hid, 128), F32),
            pltpu.VMEM((blocks, lines * width, 1), F32),
        ],
        compiler_params=grant(22),
        cost_estimate=cost(11),
        name="mlp",
    )(me, *conv, *ct, *ct, *small)


def norm_kernel(peers, count, core_ref, *refs):
    dn_ref, stand_ref, inv_ref, vec_ref, vecx_ref, q_ref, scale_ref, small_ref = refs[:8]
    got = refs[8 : 8 + peers]
    got_small = refs[8 + peers : 9 + 3 * peers]
    (own_ref, send_ref, edge_own_ref, edge_send_ref, sums_ref, sums_send_ref, buf, gain_ref, fold_ref) = refs[9 + 3 * peers :]
    core = core_ref[0] & 1
    steps = inv_ref.shape[0]
    both = dn_ref.shape[0] // steps
    local = both // 2
    channels = both * (peers + 1)
    mine = pl.ds(pl.multiple_of(core * local, 16), local)
    theirs = pl.ds(pl.multiple_of((1 - core) * local, 16), local)
    last = pl.ds(vec_ref.shape[0] - 16, 16)
    gain_ref[mine, :] = column(vector_of(vec_ref[last, :], count)[0])[:local]
    gain_ref[theirs, :] = column(vector_of(vecx_ref[last, :], count)[0])[:local]
    shift_acc = jnp.zeros((both, 128), F32)
    gain_acc = jnp.zeros((both, 128), F32)
    for i in range(steps):
        rows = pl.ds(i * both, both)
        dn = dn_ref[rows, :]
        q = q_ref[i]
        for p in range(peers):
            start = i * (both + 16)
            dn = dn + got[p][0, pl.ds(start, both), :].astype(F32)
            extra = got[p][0, pl.ds(start + both, 16), :].astype(F32)
            q = q + (extra[0:2] + extra[2:4])
        q = q / channels
        stand = stand_ref[rows, :]
        prod = dn * stand
        shift_acc += dn[:, :128] + dn[:, 128:]
        gain_acc += prod[:, :128] + prod[:, 128:]
        buf[i] = inv_ref[i] * (dn * gain_ref[...] - q[0:1] - stand * q[1:2])
    for i in range(steps):
        own_ref[i] = buf[i, mine, :].astype(BF)
        send_ref[i] = buf[i, theirs, :].astype(BF)
    for i in range(3):
        edge_own_ref[i] = buf[i + core, mine, :].astype(BF)
        edge_send_ref[i] = buf[i + core, theirs, :].astype(BF)
    ones = jnp.ones((8, 128), F32)
    fold_ref[0], fold_ref[1] = shift_acc, gain_acc
    small = small_ref[0]
    for got_ref in got_small:
        small = small + got_ref[...]
    start = scale_ref.shape[1] - 128
    lines = [small[:1] / scale_ref[:, start : start + local], small[1:5]]
    for rows, out, rest in (
        (mine, sums_ref, lines), (theirs, sums_send_ref, [jnp.zeros((5, local), F32)])):
        pair = [
            lax.dot_general(ones, fold_ref[k, rows, :], NT, preferred_element_type=F32, precision=HI)[:1]
            for k in range(2)
        ]
        out[...] = jnp.concatenate(pair + rest + [jnp.zeros((1, local), F32)], axis=0)


def norm_backward(core, count, dn, stand, inv, vector, vector_x, q, scale, small, got, got_small):
    steps, _, width = inv.shape
    both = dn.shape[0] // steps
    local = both // 2
    return pl.pallas_call(
        functools.partial(norm_kernel, len(got), count),
        out_shape=[
            jax.ShapeDtypeStruct((steps, local, width), BF),
            jax.ShapeDtypeStruct((steps, local, width), BF),
            jax.ShapeDtypeStruct((3, local, width), BF),
            jax.ShapeDtypeStruct((3, local, width), BF),
            jax.ShapeDtypeStruct((8, local), F32),
            jax.ShapeDtypeStruct((8, local), F32),
        ],
        in_specs=[SMEM] + [VMEM] * (8 + len(got) + len(got_small)),
        out_specs=[VMEM] * 6,
        scratch_shapes=[
            pltpu.VMEM((steps, both, width), F32),
            pltpu.VMEM((both, 1), F32),
            pltpu.VMEM((2, both, 128), F32),
        ],
        compiler_params=grant(5),
        cost_estimate=cost(1.3),
        name="norm_backward",
    )(core, dn, stand, inv, vector, vector_x, q, scale, small, *got, *got_small)


def fill_tile(rows_ref, own_ref, other_ref, core, local):
    half = own_ref.shape[0]
    for part in range(2):
        lanes = slice(part * 128, part * 128 + 128)
        for i in range(half):
            rows_ref[part, pl.ds(pl.multiple_of((core * half + i) * local, 8), local), :] = (
                own_ref[i, :, lanes].astype(F32))
            rows_ref[part, pl.ds(pl.multiple_of(((1 - core) * half + i) * local, 8), local), :] = (
                other_ref[i, :, lanes].astype(F32))


def kernel_grad_kernel(core_ref, own_ref, other_ref, image_ref, sums_ref, sums_got_ref, dkernel_ref, rows_ref,
                       corr_ref, line_ref):
    local, _, width = image_ref.shape
    height = 2 * own_ref.shape[0]
    count = 7 * height
    span = 16 * SLOTS
    fill_tile(rows_ref, own_ref, other_ref, core_ref[0] & 1, local)
    lane = lax.broadcasted_iota(jnp.int32, (count, span), 1) // SLOTS
    inner_slot = lax.broadcasted_iota(jnp.int32, (7, 128), 1) % SLOTS

    def body(g, carry):
        images = image_ref[pl.ds(g * 16, 16)].reshape(span, width)
        corr = jnp.zeros((count, span), F32)
        for inner in range(16):
            a = rows_ref[0, pl.ds(g * 16 + inner, height, stride=local), :]
            b = rows_ref[1, pl.ds(g * 16 + inner, height, stride=local), :]
            stack = jnp.concatenate(
                [jnp.concatenate(shift_halves(a, b, 3 - s), axis=1) for s in range(7)], axis=0)
            value = lax.dot_general(stack.astype(BF), images, NT, preferred_element_type=F32)
            corr = jnp.where(lane == inner, value, corr)
        for part in range(2):
            lanes = slice(part * 128, part * 128 + 128)
            corr_ref[part] = corr[:, lanes]
            line = corr_ref[part, pl.ds(0, 7, stride=height), :]
            for h in range(1, height):
                value = corr_ref[part, pl.ds(h, 7, stride=height), :]
                line = line + jnp.where(
                    inner_slot < SLOTS - h, pltpu.roll(value, 128 - h, 1), pltpu.roll(value, SLOTS - h, 1))
            line_ref[part, g, pl.ds(0, 7), :] = line
        return carry

    lax.fori_loop(0, local // 16, body, 0)
    slot = lax.broadcasted_iota(jnp.int32, (7, span), 1) % SLOTS
    total = jnp.zeros(dkernel_ref.shape, F32)
    for g in range(local // 16):
        lines = jnp.concatenate([line_ref[p, g, pl.ds(0, 7), :] for p in range(2)], axis=1)
        spread = [jnp.where(slot == (r - 3) % SLOTS, lines, 0.0) for r in range(7)] + [jnp.zeros((7, span), F32)]
        pick = (lax.broadcasted_iota(jnp.int32, (local, span), 0) - g * 16
                == lax.broadcasted_iota(jnp.int32, (local, span), 1) // SLOTS).astype(F32)
        total = total + lax.dot_general(
            jnp.concatenate(spread, axis=0), pick, NT, preferred_element_type=F32, precision=HI)
    dkernel_ref[...] = total * grad_scale
    sums = (sums_ref[...] + sums_got_ref[...]) * grad_scale
    dkernel_ref[pl.ds(49, 7), :] = sums[:7]


def kernel_grad(core, own, other, image16, sums, sums_got):
    local = image16.shape[0]
    height = 2 * own.shape[0]
    return pl.pallas_call(
        kernel_grad_kernel,
        out_shape=jax.ShapeDtypeStruct((56, local), F32),
        in_specs=[SMEM] + [VMEM] * 5,
        out_specs=VMEM,
        scratch_shapes=[
            pltpu.VMEM((2, height * local, 128), F32),
            pltpu.VMEM((2, 7 * height, 128), F32),
            pltpu.VMEM((2, local // 16, 8, 128), F32),
        ],
        compiler_params=grant(5),
        cost_estimate=cost(4),
        name="kernel_grad",
    )(core, own, other, image16, sums, sums_got)


def image_grad_kernel(core_ref, own_ref, other_ref, same_ref, cross_ref, ct_ref, taps_ref, out_ref, rows_ref):
    local, height, width = ct_ref.shape
    core = core_ref[0] & 1
    count = 7 * height
    fill_tile(rows_ref, own_ref, other_ref, core, local)
    for part in range(2):
        lanes = slice(part * 128, part * 128 + 128)
        for i in range(3):
            a = pl.multiple_of((height + 5 * core + i) * local, 8)
            b = pl.multiple_of((height + 5 * (1 - core) + i) * local, 8)
            rows_ref[part, pl.ds(a, local), :] = same_ref[i, :, lanes].astype(F32)
            rows_ref[part, pl.ds(b, local), :] = cross_ref[i, :, lanes].astype(F32)
        rows_ref[part, pl.ds((height + 3) * local, 2 * local), :] = jnp.zeros((2 * local, 128), F32)

    def body(g, carry):
        tiles = []
        for u in range(8):
            pair = [rows_ref[p, pl.ds(g * 8 + u, SLOTS, stride=local), :] for p in range(2)]
            tiles.append(jnp.concatenate(pair, axis=1))
        right = jnp.concatenate(tiles, axis=0).astype(BF)
        start = pl.multiple_of(g * 8 * count, 16)
        products = jnp.dot(taps_ref[pl.ds(start, 8 * count), :], right, preferred_element_type=F32)
        for u in range(8):
            ch = g * 8 + u
            left_right = shift_sum(products[u * count : (u + 1) * count], height, -1)
            out_ref[ch] = (ct_ref[ch].astype(F32) + jnp.concatenate(left_right, axis=1)).astype(BF)
        return carry

    lax.fori_loop(0, local // 8, body, 0)


def image_grad(core, own, other, same, cross, ct, taps):
    local, height, width = ct.shape
    return pl.pallas_call(
        image_grad_kernel,
        out_shape=jax.ShapeDtypeStruct((local, height, width), BF),
        in_specs=[SMEM] + [VMEM] * 6,
        out_specs=VMEM,
        scratch_shapes=[pltpu.VMEM((2, SLOTS * local, 128), F32)],
        compiler_params=grant(6),
        cost_estimate=cost(5),
        name="image_grad",
    )(core, own, other, same, cross, ct, taps)


def finish_kernel(blocks, core_ref, image_ref, vector_ref, sums_ref, sums_got_ref, *refs):
    part_refs = refs[:blocks]
    out_ref, dkernel_ref, shift_ref, gain_ref, scale_ref, bias_ref, rows_ref, col_ref = refs[blocks:]
    sums = sums_ref[...] + sums_got_ref[...]
    dkernel_ref[...] = sums[:49]
    shift_ref[...], gain_ref[...], scale_ref[...] = sums[49:50], sums[50:51], sums[51:52]
    bias_ref[...] = jnp.concatenate([sums[52 + i : 53 + i] for i in range(4)], axis=1)
    local, height, width = image_ref.shape
    half = height // 2
    core = core_ref[0] & 1
    col_ref[...] = column(vector_ref[...])
    scale = col_ref[pl.ds(vector_ref.shape[1] - 128, local), :]
    for which in range(2):
        place = core if which == 0 else 1 - core
        for i in range(half):
            rows = pl.ds(i * local, local)
            total = part_refs[which][rows, :].astype(F32)
            for k in range(which + 2, blocks, 2):
                total = total + part_refs[k][rows, :].astype(F32)
            total = total * scale
            start = pl.multiple_of((place * half + i) * local, 8)
            for part in range(2):
                rows_ref[part, pl.ds(start, local), :] = total[:, part * 128 : part * 128 + 128]

    def body(g, carry):
        for u in range(8):
            ch = g * 8 + u
            pair = [rows_ref[p, pl.ds(ch, height, stride=local), :] for p in range(2)]
            out_ref[ch] = (image_ref[ch].astype(F32) + jnp.concatenate(pair, axis=1)).astype(BF)
        return carry

    lax.fori_loop(0, local // 8, body, 0)


def finish(core, image, vector, sums, sums_got, parts):
    local, height, width = image.shape
    return pl.pallas_call(
        functools.partial(finish_kernel, len(parts)),
        out_shape=[
            jax.ShapeDtypeStruct((local, height, width), BF),
            jax.ShapeDtypeStruct((49, local), F32),
            *[jax.ShapeDtypeStruct((1, local), F32)] * 3,
            jax.ShapeDtypeStruct((1, 4 * local), F32),
        ],
        in_specs=[SMEM] + [VMEM] * (4 + len(parts)),
        out_specs=[VMEM] * 6,
        scratch_shapes=[
            pltpu.VMEM((2, height * local, 128), F32),
            pltpu.VMEM((vector.shape[1], 1), F32),
        ],
        compiler_params=grant(5),
        cost_estimate=cost(2),
        name="finish",
    )(core, image, vector, sums, sums_got, *parts)


def swap(value, axis, size, k):
    return lax.ppermute(value, axis, [(i, i ^ k) for i in range(size)])


def after(value, *gates):
    return lax.optimization_barrier((value, *gates))[0]


def sum_over_space(value, size):
    k = 1
    while 2 * k < size:
        value = value + swap(value, "space", size, k)
        k *= 2
    return value, swap(value, "space", size, k)


def scatter_over_space(ids, own, got, size):
    if size > 4:
        total = (own.astype(F32) + got.astype(F32)).astype(BF)
        return lax.psum_scatter(total, "space", scatter_dimension=1, tiled=True).astype(F32), total
    mine, *others = merge(ids, own, got, size)
    moved = [swap(p, "space", size, k + 1) for k, p in enumerate(others)]
    return mine + sum(m.astype(F32) for m in moved), mine


def per_device(image, dw_weight, ln_gain, ln_shift, w_in, b_in, w_out, layer_scale, cotangent):
    local, height, width = image.shape
    hid = w_in.shape[1]
    n_chan, n_space = lax.axis_size("chan"), lax.axis_size("space")
    ids = jnp.stack([lax.axis_index("chan"), lax.axis_index("space")]).astype(jnp.int32)

    used = 2 * local + hid + 128
    count = -(-used // width)
    packed = jnp.pad(jnp.concatenate([ln_gain, ln_shift, b_in]), (0, count * width - used))
    packed = jnp.concatenate([packed, jnp.pad(layer_scale, (0, 128 - local))])[None]
    d_mine, d_theirs = pack(ids, cotangent, packed)
    d_all = [d_mine] + [
        swap(d_theirs if k % 2 else d_mine, "chan", n_chan, k) for k in range(1, n_chan)
    ]
    pairs_a = [(s, s ^ 1) for s in range(n_space) if s ^ 1 < n_space]
    pairs_b = [(s, t) for s in range(n_space) for t in [s + 1 if s % 2 else s - 1] if 0 <= t < n_space]
    edge_a, edge_b = edges(ids, after(image, d_mine))
    got_a = lax.ppermute(edge_a, "space", pairs_a)
    got_b = lax.ppermute(edge_b, "space", pairs_b)
    dw_weight, w_in, w_out = lax.optimization_barrier((dw_weight, w_in, w_out, edge_a))[:3]
    w_inx = swap(w_in, "chan", n_chan, 1)
    w_outx = swap(w_out, "chan", n_chan, 1)
    weight = jnp.pad(dw_weight.T, ((0, 15), (0, -local % 128)))
    taps = make_taps(weight, local, height, False)
    taps, d_all = lax.optimization_barrier((taps, d_all))

    mine, theirs, image16 = conv_forward(ids, image, got_a, got_b, taps)
    conv = [mine] + [swap(theirs if k % 2 else mine, "chan", n_chan, k) for k in range(1, n_chan)]
    w_in, w_inx, w_out, w_outx, weight = lax.optimization_barrier((w_in, w_inx, w_out, w_outx, weight, mine))[:5]
    w_int, w_intx, w_outt, w_outtx = turn(w_in, w_inx, w_out, w_outx)
    taps_back = make_taps(weight, local, height, True)
    weights = [w_in, w_inx, w_int, w_intx, w_out, w_outx, w_outt, w_outtx]
    conv[0] = after(conv[0], taps_back)
    branch, dn_send, dn, stand, inv, q, dw, dw_send, small = mlp(ids, conv, d_all, count, weights)

    got = [swap(dn_send[k - 1 : k], "chan", n_chan, 2 * k) for k in range(1, n_chan // 2)]
    dw, gate = scatter_over_space(ids, dw, swap(dw_send, "chan", n_chan, 1), n_space)
    dw = dw * grad_scale
    inv = after(inv, gate)
    got_small = [swap(small[k], "chan", n_chan, k) for k in range(1, n_chan)]

    dconv, dconv_send, edge, edge_send, sums, sums_send = norm_backward(
        ids, count, dn, stand, inv, d_all[0], d_all[1], q, packed, small, got, got_small)
    same_pairs, cross_pairs = [], []
    for s in range(n_space):
        for c in range(n_chan):
            t = s + 1 if c % 2 else s - 1
            if 0 <= t < n_space:
                same_pairs.append((s * n_chan + c, t * n_chan + c))
                cross_pairs.append((s * n_chan + c, t * n_chan + (c ^ 1)))
    same = lax.ppermute(edge, ("space", "chan"), same_pairs)
    cross = lax.ppermute(edge_send, ("space", "chan"), cross_pairs)
    other = swap(dconv_send, "chan", n_chan, 1)
    sums_got = swap(sums_send, "chan", n_chan, 1)
    branch = after(branch, other)
    parts = [branch[0]] + [swap(branch[k], "chan", n_chan, k) for k in range(1, n_chan)]

    sums, sums_got = sum_over_space(kernel_grad(ids, dconv, other, image16, sums, sums_got), n_space)
    d_image = image_grad(ids, dconv, other, same, cross, cotangent, taps_back)
    output, d_kernel, d_shift, d_gain, d_scale, d_b_in = finish(ids, image, packed, sums, sums_got, parts)
    return (output, d_image, d_kernel.T, d_gain[0], d_shift[0], dw[0], d_b_in[0], dw[1].T, d_scale[0])


def solution(mesh):
    return jax.shard_map(
        per_device,
        mesh=mesh,
        in_specs=(
            P("chan", ("groups", "space"), None),
            P("chan", None),
            P("chan"),
            P("chan"),
            P(None, "chan"),
            P("chan"),
            P("chan", None),
            P("chan"),
            P("chan", ("groups", "space"), None),
        ),
        out_specs=(
            P("chan", ("groups", "space"), None),
            P("chan", ("groups", "space"), None),
            P("chan", "groups"),
            P(("groups", "chan")),
            P(("groups", "chan")),
            P("space", ("groups", "chan")),
            P(("groups", "chan")),
            P(("groups", "chan"), "space"),
            P(("groups", "chan")),
        ),
        check_vma=False,
    )
```

```python
import functools

import jax
import jax.numpy as jnp
from jax import lax
from jax.experimental import pallas as pl
from jax.experimental.pallas import tpu as pltpu
from jax.sharding import PartitionSpec as P

BF = jnp.bfloat16
F32 = jnp.float32
grad_scale = 1.0 / 128.0
SLOTS = 16
VMEM = pl.BlockSpec(memory_space=pltpu.VMEM)
SMEM = pl.BlockSpec(memory_space=pltpu.SMEM)


def cost(microseconds):
    return pl.CostEstimate(flops=int(microseconds * 1.1e9), bytes_accessed=0, transcendentals=0)


def grant(mib):
    return pltpu.CompilerParams(vmem_limit_bytes=mib << 20)


HI = lax.Precision.HIGHEST
NT = (((1,), (1,)), ((), ()))


def column(row):
    return jnp.broadcast_to(row, (8, row.shape[1])).T[:, :1]


def shift_halves(a, b, by):
    if by == 0:
        return a, b
    lane = lax.broadcasted_iota(jnp.int32, a.shape, 1)
    k = (-by) % 128
    ra, rb = pltpu.roll(a, k, 1), pltpu.roll(b, k, 1)
    if by > 0:
        inner = lane < 128 - by
        return jnp.where(inner, ra, rb), jnp.where(inner, rb, 0.0)
    inner = lane >= -by
    return jnp.where(inner, ra, 0.0), jnp.where(inner, rb, ra)


def taps_kernel(flip, height, weight_ref, out_ref, rows_ref):
    local = out_ref.shape[0] // (7 * height)
    count = 7 * height
    tap = lax.broadcasted_iota(jnp.int32, (64, 128), 0)
    slot = lax.broadcasted_iota(jnp.int32, (64, 128), 1) % SLOTS
    row = jnp.where(slot < height + 3, slot, slot - SLOTS)
    weight = weight_ref[...].astype(F32).T[:local].astype(BF)
    for h in range(height):
        r = h + 3 - row if flip else row - h + 3
        base = jnp.where((r >= 0) & (r < 7) & (row >= -3), 7 * r, -100)
        for s in range(7):
            table = (tap == base + s).astype(F32).astype(BF)
            rows_ref[pl.ds((s * height + h) * local, local), :] = jnp.dot(
                weight, table, preferred_element_type=F32)
    lane = lax.broadcasted_iota(jnp.int32, (count, 128), 1) // SLOTS

    def body(g, carry):
        for u in range(0, 8, 2):
            pair = [
                jnp.where(lane == u + v, rows_ref[pl.ds(g * 8 + u + v, count, stride=local), :], 0.0)
                for v in range(2)
            ]
            start = pl.multiple_of((g * 8 + u) * count, 16)
            out_ref[pl.ds(start, 2 * count), :] = jnp.concatenate(pair, axis=0).astype(BF)
        return carry

    lax.fori_loop(0, local // 8, body, 0, unroll=6)


def make_taps(weight, local, height, flip):
    count = 7 * height
    return pl.pallas_call(
        functools.partial(taps_kernel, flip, height),
        out_shape=jax.ShapeDtypeStruct((local * count, 128), BF),
        in_specs=[VMEM],
        out_specs=VMEM,
        scratch_shapes=[pltpu.VMEM((count * local, 128), F32)],
        compiler_params=grant(6),
        cost_estimate=cost(2.4),
        name="taps_back" if flip else "taps_forward",
    )(weight)


def vector_of(lines, count):
    lines = lines.astype(F32)
    return [
        lines[r : r + 1] + lines[count + r : count + r + 1] + lines[2 * count + r : 2 * count + r + 1]
        for r in range(count)
    ]


def edge_kernel(ids_ref, image_ref, edge_a_ref, edge_b_ref, rows_ref):
    local, height, width = image_ref.shape
    odd = ids_ref[1] & 1

    def body(g, carry):
        for u in range(8):
            tile = image_ref[g * 8 + u].astype(F32)
            for part in range(2):
                rows_ref[part, pl.ds(g * 8 + u, height, stride=local), :] = tile[:, part * 128 : part * 128 + 128]
        return carry

    lax.fori_loop(0, local // 8, body, 0, unroll=6)
    top, bottom = (0, (height - 3) * local)
    for part in range(2):
        lanes = slice(part * 128, part * 128 + 128)
        to_a = pl.multiple_of(jnp.where(odd == 0, bottom, top), 16)
        to_b = pl.multiple_of(jnp.where(odd == 0, top, bottom), 16)
        edge_a_ref[:, lanes] = rows_ref[part, pl.ds(to_a, 3 * local), :].astype(BF)
        edge_b_ref[:, lanes] = rows_ref[part, pl.ds(to_b, 3 * local), :].astype(BF)


def edges(ids, image):
    local, height, width = image.shape
    return pl.pallas_call(
        edge_kernel,
        out_shape=[jax.ShapeDtypeStruct((3 * local, width), BF)] * 2,
        in_specs=[SMEM, VMEM],
        out_specs=[VMEM, VMEM],
        scratch_shapes=[pltpu.VMEM((2, height * local, 128), F32)],
        compiler_params=grant(3),
        cost_estimate=cost(1.2),
        name="edges",
    )(ids, image)


def pack_kernel(ids_ref, ct_ref, vector_ref, own_ref, send_ref, rows_ref, col_ref):
    local, height, width = ct_ref.shape
    core = ids_ref[0] & 1
    vector = vector_ref[...]
    count = vector.shape[1] // width
    col_ref[...] = column(vector)
    scale = col_ref[pl.ds(vector.shape[1] - 128, local), :]
    high = vector.astype(BF).astype(F32)
    middle = (vector - high).astype(BF).astype(F32)
    low = vector - high - middle
    lines = [part[:, r * width : r * width + width] for part in (high, middle, low) for r in range(count)]
    lines = jnp.concatenate(lines + [jnp.zeros((16 - 3 * count, width), F32)], axis=0).astype(BF)
    own_ref[pl.ds(height // 2 * local, 16), :] = lines
    send_ref[pl.ds(height // 2 * local, 16), :] = lines

    def body(g, carry):
        for u in range(8):
            tile = ct_ref[g * 8 + u].astype(F32)
            for part in range(2):
                rows_ref[part, pl.ds(g * 8 + u, height, stride=local), :] = tile[:, part * 128 : part * 128 + 128]
        return carry

    lax.fori_loop(0, local // 8, body, 0, unroll=6)
    for i in range(height // 2):
        rows = pl.ds(i * local, local)
        mine = pl.multiple_of((core * (height // 2) + i) * local, 16)
        theirs = pl.multiple_of(((1 - core) * (height // 2) + i) * local, 16)
        for part in range(2):
            lanes = slice(part * 128, part * 128 + 128)
            own_ref[rows, lanes] = (rows_ref[part, pl.ds(mine, local), :] * scale).astype(BF)
            send_ref[rows, lanes] = (rows_ref[part, pl.ds(theirs, local), :] * scale).astype(BF)


def pack(ids, ct, vector):
    local, height, width = ct.shape
    return pl.pallas_call(
        pack_kernel,
        out_shape=[jax.ShapeDtypeStruct((height // 2 * local + 16, width), BF)] * 2,
        in_specs=[SMEM, VMEM, VMEM],
        out_specs=[VMEM, VMEM],
        scratch_shapes=[
            pltpu.VMEM((2, height * local, 128), F32),
            pltpu.VMEM((vector.shape[1], 1), F32),
        ],
        compiler_params=grant(4),
        cost_estimate=cost(1.4),
        name="pack",
    )(ids, ct, vector)


def turn_kernel(*refs):
    for source, out in zip(refs[:4], refs[4:]):
        out[...] = source[...].T


def turn(*weights):
    return pl.pallas_call(
        turn_kernel,
        out_shape=[jax.ShapeDtypeStruct(w.shape[::-1], BF) for w in weights],
        in_specs=[VMEM] * 4,
        out_specs=[VMEM] * 4,
        compiler_params=grant(5),
        cost_estimate=cost(0.4),
        name="turn",
    )(*weights)


def merge_kernel(ids_ref, own_ref, got_ref, mine_ref, *rest):
    outs, buf = rest[:-1], rest[-1]
    rows = mine_ref.shape[1]
    me = ids_ref[1]
    for p in range(2):
        buf[...] = own_ref[p].astype(F32) + got_ref[p].astype(F32)
        mine_ref[p] = buf[pl.ds(pl.multiple_of(me * rows, 8), rows), :]
        for k, out in enumerate(outs):
            out[p] = buf[pl.ds(pl.multiple_of((me ^ (k + 1)) * rows, 8), rows), :].astype(BF)


def merge(ids, own, got, size):
    rows, hid = own.shape[1] // size, own.shape[2]
    return pl.pallas_call(
        merge_kernel,
        out_shape=[jax.ShapeDtypeStruct((2, rows, hid), F32)]
        + [jax.ShapeDtypeStruct((2, rows, hid), BF)] * (size - 1),
        in_specs=[SMEM, VMEM, VMEM],
        out_specs=[VMEM] * size,
        scratch_shapes=[pltpu.VMEM(own.shape[1:], F32)],
        compiler_params=grant(5),
        cost_estimate=cost(1),
        name="merge",
    )(ids, own, got)


def shift_sum(products, height, sign):
    left = products[3 * height : 4 * height, :128]
    right = products[3 * height : 4 * height, 128:]
    for s in (0, 1, 2, 4, 5, 6):
        block = products[s * height : (s + 1) * height]
        a, b = shift_halves(block[:, :128], block[:, 128:], sign * (s - 3))
        left, right = left + a, right + b
    return left, right


def conv_kernel(ids_ref, image_ref, got_a_ref, got_b_ref, taps_ref, own_ref, send_ref, image16_ref, acc_ref, rim_ref):
    local, height, width = image_ref.shape
    rows = own_ref.shape[0]
    count = 7 * height
    core, odd = ids_ref[0] & 1, ids_ref[1] & 1
    for part in range(2):
        lanes = slice(part * 128, part * 128 + 128)
        to_a = pl.multiple_of(5 * odd * local, 16)
        to_b = pl.multiple_of(5 * (1 - odd) * local, 16)
        rim_ref[part, pl.ds(to_a, 3 * local), :] = got_a_ref[:, lanes].astype(F32)
        rim_ref[part, pl.ds(to_b, 3 * local), :] = got_b_ref[:, lanes].astype(F32)
        rim_ref[part, pl.ds(3 * local, 2 * local), :] = jnp.zeros((2 * local, 128), F32)

    def body(g, carry):
        for u in range(8):
            ch = g * 8 + u
            pair = [rim_ref[p, pl.ds(ch, SLOTS - height, stride=local), :] for p in range(2)]
            tile = jnp.concatenate([image_ref[ch].astype(F32), jnp.concatenate(pair, axis=1)], axis=0)
            image16_ref[ch] = tile.astype(BF)
        right = image16_ref[pl.ds(g * 8, 8)].reshape(8 * SLOTS, width)
        taps = taps_ref[pl.ds(pl.multiple_of(g * 8 * count, 16), 8 * count), :]
        products = jnp.dot(taps, right, preferred_element_type=F32)
        for u in range(8):
            pair = shift_sum(products[u * count : (u + 1) * count], height, 1)
            for half in range(2):
                acc_ref[half, pl.ds(g * 8 + u, height, stride=local), :] = pair[half]
        return carry

    lax.fori_loop(0, local // 8, body, 0, unroll=6)
    for half in range(2):
        lanes = slice(half * 128, half * 128 + 128)
        mine = pl.multiple_of(core * rows, 16)
        theirs = pl.multiple_of((1 - core) * rows, 16)
        own_ref[:, lanes] = acc_ref[half, pl.ds(mine, rows), :].astype(BF)
        send_ref[:, lanes] = acc_ref[half, pl.ds(theirs, rows), :].astype(BF)


def conv_forward(ids, image, got_a, got_b, taps):
    local, height, width = image.shape
    rows = height // 2 * local
    return pl.pallas_call(
        conv_kernel,
        out_shape=[jax.ShapeDtypeStruct((rows, width), BF)] * 2
        + [jax.ShapeDtypeStruct((local, SLOTS, width), BF)],
        in_specs=[SMEM] + [VMEM] * 4,
        out_specs=[VMEM] * 3,
        scratch_shapes=[
            pltpu.VMEM((2, height * local, 128), F32),
            pltpu.VMEM((2, (SLOTS - height) * local, 128), F32),
        ],
        compiler_params=grant(6),
        cost_estimate=cost(5),
        name="conv_forward",
    )(ids, image, got_a, got_b, taps)


def mlp_kernel(blocks, count, me_ref, *refs):
    conv_refs = refs[:blocks]
    ct_refs = refs[blocks : 2 * blocks]
    (w_in_ref, w_inx_ref, w_int_ref, w_intx_ref, w_out_ref, w_outx_ref,
     w_outt_ref, w_outtx_ref) = refs[2 * blocks : 2 * blocks + 8]
    (branch_ref, dn_ref, dn_own_ref, stand_ref, inv_ref, q_ref, dw_ref, dwx_ref, small_ref,
     normed, dbranch, active, dhalf, centred, fold_ref, rounded, bias_ref, gain_ref, shift_ref,
     b_ref) = refs[2 * blocks + 8 :]
    me = me_ref[0]
    steps, _, width = inv_ref.shape
    hid = w_in_ref.shape[1]
    channels = w_in_ref.shape[0]
    local = channels // blocks

    def where(j):
        return pl.ds(pl.multiple_of((me ^ j) * local, 16), local)

    def chip(k):
        return pl.ds(pl.multiple_of(((me // 2) ^ k) * 2 * local, 16), 2 * local)

    def wide(value):
        return jnp.concatenate([value, value], axis=1)

    for j in range(blocks):
        lines = vector_of(ct_refs[j][pl.ds(steps * local, 16), :], count)
        cols = jnp.concatenate([column(line) for line in lines], axis=0)
        gain_ref[where(j), :] = jnp.broadcast_to(cols[:local], (local, 128))
        shift_ref[where(j), :] = jnp.broadcast_to(cols[local : 2 * local], (local, 128))
        if j < 2:
            b_ref[j] = jnp.broadcast_to(cols[2 * local : 2 * local + hid], (hid, 128))

    k0, k1 = (0.7978845608028654, 0.044715)
    parts = ((w_in_ref, w_int_ref, w_out_ref, w_outt_ref),
             (w_inx_ref, w_intx_ref, w_outx_ref, w_outtx_ref))
    for i in range(steps):
        rows = pl.ds(i * local, local)
        pixels = slice(i * width, i * width + width)
        for j in range(blocks):
            rounded[where(j), :] = conv_refs[j][rows, :]
            dbranch[where(j), pixels] = ct_refs[j][rows, :]
        value = rounded[...].astype(F32)
        average = jnp.sum(value, axis=0, keepdims=True) / channels
        value = value - average
        variance = jnp.sum(value * value, axis=0, keepdims=True) / channels
        inv_std = lax.rsqrt(variance + 1e-06)
        inv_ref[i] = inv_std
        stand = value * inv_std
        centred[...] = stand
        normed[:, pixels] = (stand * wide(gain_ref[...]) + wide(shift_ref[...])).astype(BF)
        stand_ref[pl.ds(i * 2 * local, 2 * local), :] = centred[chip(0), :]
        x = normed[:, pixels]
        d = dbranch[:, pixels]
        branch, dnormed = None, None
        for part, (w_in, w_int, w_out, w_outt) in enumerate(parts):
            pre = jnp.dot(w_int[...], x, preferred_element_type=F32) + wide(b_ref[part])
            dact = jnp.dot(w_out[...], d, preferred_element_type=F32)
            square = pre * pre
            th = jnp.tanh(pre * (k0 + (k0 * k1) * square))
            half = 0.5 * pre
            active[part, :, pixels] = (half + half * th).astype(BF)
            slope = 0.5 + 0.5 * th + half * (1.0 - th * th) * (k0 + (3.0 * k0 * k1) * square)
            dpre = dact * slope
            bias = dpre[:, :128] + dpre[:, 128:]
            bias_ref[part] = bias if i == 0 else bias_ref[part] + bias
            dhalf[part, :, pixels] = dpre.astype(BF)
            b_part = jnp.dot(w_outt[...], active[part, :, pixels], preferred_element_type=F32)
            d_part = jnp.dot(w_in[...], dhalf[part, :, pixels], preferred_element_type=F32)
            branch = b_part if part == 0 else branch + b_part
            dnormed = d_part if part == 0 else dnormed + d_part
        rounded[...] = branch.astype(BF)
        for j in range(blocks):
            branch_ref[j, rows, :] = rounded[where(j), :]
        scaled = dnormed * wide(gain_ref[...])
        first = jnp.sum(scaled, axis=0, keepdims=True)
        second = jnp.sum(scaled * centred[...], axis=0, keepdims=True)
        centred[...] = dnormed
        dn_own_ref[pl.ds(i * 2 * local, 2 * local), :] = centred[chip(0), :]
        q = jnp.concatenate([first, second], axis=0)
        q_ref[i] = q
        high = q.astype(BF).astype(F32)
        start = i * (2 * local + 16)
        extra = jnp.concatenate([high, q - high, jnp.zeros((12, width), F32)], axis=0).astype(BF)
        for k in range(1, blocks // 2):
            dn_ref[k - 1, pl.ds(start, 2 * local), :] = centred[chip(k), :].astype(BF)
            dn_ref[k - 1, pl.ds(start + 2 * local, 16), :] = extra

    ones = jnp.ones((8, 128), F32)

    def lane_sums(value):
        return lax.dot_general(ones, value, NT, preferred_element_type=F32, precision=HI)[:1]

    prod = None
    for part, out in ((0, dw_ref), (1, dwx_ref)):
        out[0] = lax.dot_general(normed[...], dhalf[part], NT, preferred_element_type=F32).astype(BF)
        d_out = lax.dot_general(dbranch[...], active[part], NT, preferred_element_type=F32)
        out[1] = d_out.astype(BF)
        term = d_out * parts[part][3][...].astype(F32)
        prod = term if part == 0 else prod + term
    if hid % 128:
        fold_ref[...] = jnp.concatenate(
            [jnp.sum(prod, axis=1, keepdims=True), jnp.zeros((channels, 127), F32)], axis=1)
    else:
        fold_ref[...] = sum(prod[:, i : i + 128] for i in range(128, hid, 128)) + prod[:, :128]
    pad = jnp.zeros((1, width - 2 * local), F32)
    for k in range(blocks // 2):
        line = jnp.concatenate([lane_sums(fold_ref[chip(k), :]), pad], axis=1)
        if k == 0:
            scale_line = line
        else:
            high = line.astype(BF).astype(F32)
            middle = (line - high).astype(BF).astype(F32)
            q = q_ref[steps - 1]
            q_high = q.astype(BF).astype(F32)
            extra = [q_high, q - q_high, high, middle, line - high - middle, jnp.zeros((9, width), F32)]
            dn_ref[k - 1, pl.ds(dn_ref.shape[1] - 16, 16), :] = jnp.concatenate(extra, axis=0).astype(BF)
    small_ref[0] = jnp.concatenate([scale_line, jnp.zeros((7, width), F32)], axis=0)
    for part in range(2):
        lines = [lane_sums(bias_ref[part, pl.ds(r * local, local), :]) for r in range(hid // local)]
        lines = jnp.concatenate(lines + [jnp.zeros((8 - len(lines), local), F32)], axis=0)
        small_ref[1 + part] = jnp.concatenate([lines, jnp.zeros((8, width - local), F32)], axis=1)


def mlp(me, conv, ct, count, weights):
    blocks = len(conv)
    rows, width = conv[0].shape
    channels, hid = weights[0].shape
    local = channels // blocks
    steps = rows // local
    peers = max(blocks // 2 - 1, 1)
    return pl.pallas_call(
        functools.partial(mlp_kernel, blocks, count),
        out_shape=[
            jax.ShapeDtypeStruct((blocks, rows, width), BF),
            jax.ShapeDtypeStruct((peers, steps * (2 * local + 16), width), BF),
            jax.ShapeDtypeStruct((2 * rows, width), F32),
            jax.ShapeDtypeStruct((2 * rows, width), F32),
            jax.ShapeDtypeStruct((steps, 1, width), F32),
            jax.ShapeDtypeStruct((steps, 2, width), F32),
            *[jax.ShapeDtypeStruct((2, channels, hid), BF)] * 2,
            jax.ShapeDtypeStruct((3, 8, width), F32),
        ],
        in_specs=[SMEM] + [VMEM] * (2 * blocks + 8),
        out_specs=[VMEM] * 9,
        scratch_shapes=[
            pltpu.VMEM((channels, rows // local * width), BF),
            pltpu.VMEM((channels, rows // local * width), BF),
            pltpu.VMEM((2, hid, rows // local * width), BF),
            pltpu.VMEM((2, hid, rows // local * width), BF),
            pltpu.VMEM((channels, width), F32),
            pltpu.VMEM((channels, 128), F32),
            pltpu.VMEM((channels, width), BF),
            pltpu.VMEM((2, hid, 128), F32),
            pltpu.VMEM((channels, 128), F32),
            pltpu.VMEM((channels, 128), F32),
            pltpu.VMEM((2, hid, 128), F32),
        ],
        compiler_params=grant(22),
        cost_estimate=cost(8),
        name="mlp",
    )(me, *conv, *ct, *weights)


def norm_kernel(peers, count, core_ref, *refs):
    dn_ref, stand_ref, inv_ref, vec_ref, vecx_ref, q_ref, small_ref = refs[:7]
    got = refs[7 : 7 + peers]
    (own_ref, send_ref, edge_own_ref, edge_send_ref, sums_ref, buf, gain_ref, fold_ref) = refs[7 + peers :]
    core = core_ref[0] & 1
    steps = inv_ref.shape[0]
    both = dn_ref.shape[0] // steps
    local = both // 2
    channels = both * (peers + 1)
    mine = pl.ds(pl.multiple_of(core * local, 16), local)
    theirs = pl.ds(pl.multiple_of((1 - core) * local, 16), local)
    last = pl.ds(vec_ref.shape[0] - 16, 16)
    gain_ref[mine, :] = column(vector_of(vec_ref[last, :], count)[0])[:local]
    gain_ref[theirs, :] = column(vector_of(vecx_ref[last, :], count)[0])[:local]
    shift_acc = jnp.zeros((both, 128), F32)
    gain_acc = jnp.zeros((both, 128), F32)
    for i in range(steps):
        rows = pl.ds(i * both, both)
        dn = dn_ref[rows, :]
        q = q_ref[i]
        for p in range(peers):
            start = i * (both + 16)
            dn = dn + got[p][0, pl.ds(start, both), :].astype(F32)
            extra = got[p][0, pl.ds(start + both, 16), :].astype(F32)
            q = q + (extra[0:2] + extra[2:4])
        q = q / channels
        stand = stand_ref[rows, :]
        prod = dn * stand
        shift_acc += dn[:, :128] + dn[:, 128:]
        gain_acc += prod[:, :128] + prod[:, 128:]
        buf[i] = inv_ref[i] * (dn * gain_ref[...] - q[0:1] - stand * q[1:2])
    for i in range(steps):
        own_ref[i] = buf[i, mine, :].astype(BF)
        send_ref[pl.ds(i * local, local), :] = buf[i, theirs, :].astype(BF)
    for i in range(3):
        edge_own_ref[i] = buf[i + core, mine, :].astype(BF)
        edge_send_ref[i] = buf[i + core, theirs, :].astype(BF)
    ones = jnp.ones((8, 128), F32)
    fold_ref[0], fold_ref[1] = shift_acc, gain_acc
    line = small_ref[0, pl.ds(0, 1), :]
    for p in range(peers):
        extra = got[p][0, pl.ds(got[p].shape[1] - 16, 16), :].astype(F32)
        line = line + (extra[4:5] + extra[5:6] + extra[6:7])
    low, high = line[:, :local], line[:, local : 2 * local]
    scale_mine = jnp.where(core == 0, low, high)
    scale_theirs = jnp.where(core == 0, high, low)
    for rows, scale, which in ((mine, scale_mine, 1), (theirs, scale_theirs, 2)):
        pair = [
            lax.dot_general(ones, fold_ref[k, rows, :], NT, preferred_element_type=F32, precision=HI)[:1]
            for k in range(2)
        ]
        bias = small_ref[which, pl.ds(0, 4), pl.ds(0, local)]
        sums = jnp.concatenate(pair + [scale, bias, jnp.zeros((1, local), F32)], axis=0)
        if which == 1:
            sums_ref[...] = sums
        else:
            high = sums.astype(BF).astype(F32)
            middle = (sums - high).astype(BF).astype(F32)
            lines = jnp.concatenate([high, middle, sums - high - middle, jnp.zeros((8, local), F32)], axis=0)
            width = send_ref.shape[1]
            lines = jnp.concatenate([lines, jnp.zeros((32, width - local), F32)], axis=1)
            send_ref[pl.ds(steps * local, 32), :] = lines.astype(BF)


def norm_backward(core, count, dn, stand, inv, vector, vector_x, q, small, got):
    steps, _, width = inv.shape
    both = dn.shape[0] // steps
    local = both // 2
    return pl.pallas_call(
        functools.partial(norm_kernel, len(got), count),
        out_shape=[
            jax.ShapeDtypeStruct((steps, local, width), BF),
            jax.ShapeDtypeStruct((steps * local + 32, width), BF),
            jax.ShapeDtypeStruct((3, local, width), BF),
            jax.ShapeDtypeStruct((3, local, width), BF),
            jax.ShapeDtypeStruct((8, local), F32),
        ],
        in_specs=[SMEM] + [VMEM] * (7 + len(got)),
        out_specs=[VMEM] * 5,
        scratch_shapes=[
            pltpu.VMEM((steps, both, width), F32),
            pltpu.VMEM((both, 1), F32),
            pltpu.VMEM((2, both, 128), F32),
        ],
        compiler_params=grant(5),
        cost_estimate=cost(1.3),
        name="norm_backward",
    )(core, dn, stand, inv, vector, vector_x, q, small, *got)


def fill_tile(rows_ref, own_ref, other_ref, core, local):
    half = own_ref.shape[0]
    for part in range(2):
        lanes = slice(part * 128, part * 128 + 128)
        for i in range(half):
            rows_ref[part, pl.ds(pl.multiple_of((core * half + i) * local, 8), local), :] = (
                own_ref[i, :, lanes].astype(F32))
            rows_ref[part, pl.ds(pl.multiple_of(((1 - core) * half + i) * local, 8), local), :] = (
                other_ref[pl.ds(i * local, local), lanes].astype(F32))


def kernel_grad_kernel(core_ref, own_ref, other_ref, image_ref, vector_ref, sums_ref, dkernel_ref, rows_ref,
                       corr_ref, line_ref):
    local, _, width = image_ref.shape
    height = 2 * own_ref.shape[0]
    count = 7 * height
    span = 16 * SLOTS
    fill_tile(rows_ref, own_ref, other_ref, core_ref[0] & 1, local)
    lane = lax.broadcasted_iota(jnp.int32, (count, span), 1) // SLOTS
    inner_slot = lax.broadcasted_iota(jnp.int32, (7, 128), 1) % SLOTS

    def body(g, carry):
        images = image_ref[pl.ds(g * 16, 16)].reshape(span, width)
        corr = jnp.zeros((count, span), F32)
        for first in range(0, 16, 8):
            stacks = []
            for inner in range(first, first + 8):
                a = rows_ref[0, pl.ds(g * 16 + inner, height, stride=local), :]
                b = rows_ref[1, pl.ds(g * 16 + inner, height, stride=local), :]
                stacks += [jnp.concatenate(shift_halves(a, b, 3 - s), axis=1) for s in range(7)]
            stack = jnp.concatenate(stacks, axis=0).astype(BF)
            value = lax.dot_general(stack, images, NT, preferred_element_type=F32)
            for inner in range(8):
                corr = jnp.where(lane == first + inner, value[inner * count : (inner + 1) * count], corr)
        for part in range(2):
            lanes = slice(part * 128, part * 128 + 128)
            corr_ref[part] = corr[:, lanes]
            line = corr_ref[part, pl.ds(0, 7, stride=height), :]
            for h in range(1, height):
                value = corr_ref[part, pl.ds(h, 7, stride=height), :]
                line = line + jnp.where(
                    inner_slot < SLOTS - h, pltpu.roll(value, 128 - h, 1), pltpu.roll(value, SLOTS - h, 1))
            line_ref[part, g, pl.ds(0, 7), :] = line
        return carry

    lax.fori_loop(0, local // 16, body, 0, unroll=3)
    slot = lax.broadcasted_iota(jnp.int32, (7, span), 1) % SLOTS
    total = jnp.zeros(dkernel_ref.shape, F32)
    for g in range(local // 16):
        lines = jnp.concatenate([line_ref[p, g, pl.ds(0, 7), :] for p in range(2)], axis=1)
        spread = [jnp.where(slot == (r - 3) % SLOTS, lines, 0.0) for r in range(7)] + [jnp.zeros((7, span), F32)]
        pick = (lax.broadcasted_iota(jnp.int32, (local, span), 0) - g * 16
                == lax.broadcasted_iota(jnp.int32, (local, span), 1) // SLOTS).astype(F32)
        total = total + lax.dot_general(
            jnp.concatenate(spread, axis=0), pick, NT, preferred_element_type=F32, precision=HI)
    dkernel_ref[...] = total * grad_scale
    lines = other_ref[pl.ds(height // 2 * local, 32), pl.ds(0, local)].astype(F32)
    sums = (sums_ref[...] + (lines[:8] + lines[8:16] + lines[16:24])) * grad_scale
    start = vector_ref.shape[1] - 128
    scale_line = sums[2:3] / vector_ref[:, start : start + local]
    dkernel_ref[pl.ds(49, 7), :] = jnp.concatenate([sums[:2], scale_line, sums[3:7]], axis=0)


def kernel_grad(core, own, other, image16, vector, sums):
    local = image16.shape[0]
    height = 2 * own.shape[0]
    return pl.pallas_call(
        kernel_grad_kernel,
        out_shape=jax.ShapeDtypeStruct((56, local), F32),
        in_specs=[SMEM] + [VMEM] * 5,
        out_specs=VMEM,
        scratch_shapes=[
            pltpu.VMEM((2, height * local, 128), F32),
            pltpu.VMEM((2, 7 * height, 128), F32),
            pltpu.VMEM((2, local // 16, 8, 128), F32),
        ],
        compiler_params=grant(5),
        cost_estimate=cost(4),
        name="kernel_grad",
    )(core, own, other, image16, vector, sums)


def image_grad_kernel(core_ref, own_ref, other_ref, same_ref, cross_ref, ct_ref, taps_ref, out_ref, rows_ref):
    local, height, width = ct_ref.shape
    core = core_ref[0] & 1
    count = 7 * height
    fill_tile(rows_ref, own_ref, other_ref, core, local)
    for part in range(2):
        lanes = slice(part * 128, part * 128 + 128)
        for i in range(3):
            a = pl.multiple_of((height + 5 * core + i) * local, 8)
            b = pl.multiple_of((height + 5 * (1 - core) + i) * local, 8)
            rows_ref[part, pl.ds(a, local), :] = same_ref[i, :, lanes].astype(F32)
            rows_ref[part, pl.ds(b, local), :] = cross_ref[i, :, lanes].astype(F32)
        rows_ref[part, pl.ds((height + 3) * local, 2 * local), :] = jnp.zeros((2 * local, 128), F32)

    def body(g, carry):
        tiles = []
        for u in range(8):
            pair = [rows_ref[p, pl.ds(g * 8 + u, SLOTS, stride=local), :] for p in range(2)]
            tiles.append(jnp.concatenate(pair, axis=1))
        right = jnp.concatenate(tiles, axis=0).astype(BF)
        start = pl.multiple_of(g * 8 * count, 16)
        products = jnp.dot(taps_ref[pl.ds(start, 8 * count), :], right, preferred_element_type=F32)
        for u in range(8):
            ch = g * 8 + u
            left_right = shift_sum(products[u * count : (u + 1) * count], height, -1)
            out_ref[ch] = (ct_ref[ch].astype(F32) + jnp.concatenate(left_right, axis=1)).astype(BF)
        return carry

    lax.fori_loop(0, local // 8, body, 0, unroll=6)


def image_grad(core, own, other, same, cross, ct, taps):
    local, height, width = ct.shape
    return pl.pallas_call(
        image_grad_kernel,
        out_shape=jax.ShapeDtypeStruct((local, height, width), BF),
        in_specs=[SMEM] + [VMEM] * 6,
        out_specs=VMEM,
        scratch_shapes=[pltpu.VMEM((2, SLOTS * local, 128), F32)],
        compiler_params=grant(6),
        cost_estimate=cost(5),
        name="image_grad",
    )(core, own, other, same, cross, ct, taps)


def finish_kernel(blocks, core_ref, image_ref, vector_ref, sums_ref, sums_got_ref, *refs):
    part_refs = refs[:blocks]
    out_ref, dkernel_ref, shift_ref, gain_ref, scale_ref, bias_ref, rows_ref, col_ref = refs[blocks:]
    sums = sums_ref[...] + sums_got_ref[...]
    dkernel_ref[...] = sums[:49]
    shift_ref[...], gain_ref[...], scale_ref[...] = sums[49:50], sums[50:51], sums[51:52]
    bias = jnp.concatenate([sums[52 + i : 53 + i] for i in range(4)], axis=1)
    lanes = bias_ref.shape[1]
    bias_ref[...] = jnp.concatenate(
        [bias[:, i * lanes : (i + 1) * lanes] for i in range(bias_ref.shape[0])], axis=0)
    local, height, width = image_ref.shape
    half = height // 2
    core = core_ref[0] & 1
    col_ref[...] = column(vector_ref[...])
    scale = col_ref[pl.ds(vector_ref.shape[1] - 128, local), :]
    for which in range(2):
        place = core if which == 0 else 1 - core
        for i in range(half):
            rows = pl.ds(i * local, local)
            total = part_refs[which][rows, :].astype(F32)
            for k in range(which + 2, blocks, 2):
                total = total + part_refs[k][rows, :].astype(F32)
            total = total * scale
            start = pl.multiple_of((place * half + i) * local, 8)
            for part in range(2):
                rows_ref[part, pl.ds(start, local), :] = total[:, part * 128 : part * 128 + 128]

    def body(g, carry):
        for u in range(8):
            ch = g * 8 + u
            pair = [rows_ref[p, pl.ds(ch, height, stride=local), :] for p in range(2)]
            out_ref[ch] = (image_ref[ch].astype(F32) + jnp.concatenate(pair, axis=1)).astype(BF)
        return carry

    lax.fori_loop(0, local // 8, body, 0, unroll=6)


def finish(core, image, vector, sums, sums_got, parts):
    local, height, width = image.shape
    return pl.pallas_call(
        functools.partial(finish_kernel, len(parts)),
        out_shape=[
            jax.ShapeDtypeStruct((local, height, width), BF),
            jax.ShapeDtypeStruct((49, local), F32),
            *[jax.ShapeDtypeStruct((1, local), F32)] * 3,
            jax.ShapeDtypeStruct((local // 32, 128) if local % 32 == 0 else (1, 4 * local), F32),
        ],
        in_specs=[SMEM] + [VMEM] * (4 + len(parts)),
        out_specs=[VMEM] * 6,
        scratch_shapes=[
            pltpu.VMEM((2, height * local, 128), F32),
            pltpu.VMEM((vector.shape[1], 1), F32),
        ],
        compiler_params=grant(5),
        cost_estimate=cost(2),
        name="finish",
    )(core, image, vector, sums, sums_got, *parts)


def swap(value, axis, size, k):
    return lax.ppermute(value, axis, [(i, i ^ k) for i in range(size)])


def after(value, *gates):
    return lax.optimization_barrier((value, *gates))[0]


def sum_over_space(value, size):
    k = 1
    while 2 * k < size:
        value = value + swap(value, "space", size, k)
        k *= 2
    return value, swap(value, "space", size, k)


def scatter_over_space(ids, own, got, size):
    if size > 4:
        total = (own.astype(F32) + got.astype(F32)).astype(BF)
        return [lax.psum_scatter(total, "space", scatter_dimension=1, tiled=True)], total
    mine, *others = merge(ids, own, got, size)
    return [mine] + [swap(p, "space", size, k + 1) for k, p in enumerate(others)], mine


def per_device(image, dw_weight, ln_gain, ln_shift, w_in, b_in, w_out, layer_scale, cotangent):
    local, height, width = image.shape
    hid = w_in.shape[1]
    n_chan, n_space = lax.axis_size("chan"), lax.axis_size("space")
    ids = jnp.stack([lax.axis_index("chan"), lax.axis_index("space")]).astype(jnp.int32)

    used = 2 * local + hid + 128
    count = -(-used // width)
    parts = [ln_gain, ln_shift, b_in, jnp.zeros(count * width - used, F32), layer_scale, jnp.zeros(128 - local, F32)]
    packed = jnp.concatenate([v for v in parts if v.size])[None]
    d_mine, d_theirs = pack(ids, cotangent, packed)
    d_all = [d_mine] + [
        swap(d_theirs if k % 2 else d_mine, "chan", n_chan, k) for k in range(1, n_chan)
    ]
    pairs_a = [(s, s ^ 1) for s in range(n_space) if s ^ 1 < n_space]
    pairs_b = [(s, t) for s in range(n_space) for t in [s + 1 if s % 2 else s - 1] if 0 <= t < n_space]
    edge_a, edge_b = edges(ids, after(image, d_mine))
    got_a = lax.ppermute(edge_a, "space", pairs_a)
    got_b = lax.ppermute(edge_b, "space", pairs_b)
    dw_weight, w_in, w_out = lax.optimization_barrier((dw_weight, w_in, w_out, edge_a))[:3]
    w_inx = swap(w_in, "chan", n_chan, 1)
    w_outx = swap(w_out, "chan", n_chan, 1)
    weight = jnp.pad(dw_weight.T, ((0, 15), (0, -local % 128)))
    taps = make_taps(weight, local, height, False)
    taps, d_all = lax.optimization_barrier((taps, d_all))

    mine, theirs, image16 = conv_forward(ids, image, got_a, got_b, taps)
    conv = [mine] + [swap(theirs if k % 2 else mine, "chan", n_chan, k) for k in range(1, n_chan)]
    w_in, w_inx, w_out, w_outx, weight = lax.optimization_barrier((w_in, w_inx, w_out, w_outx, weight, mine))[:5]
    w_int, w_intx, w_outt, w_outtx = turn(w_in, w_inx, w_out, w_outx)
    taps_back = make_taps(weight, local, height, True)
    weights = [w_in, w_inx, w_int, w_intx, w_out, w_outx, w_outt, w_outtx]
    conv[0] = after(conv[0], taps_back)
    branch, dn_send, dn, stand, inv, q, dw, dw_send, small = mlp(ids, conv, d_all, count, weights)

    got = [swap(dn_send[k - 1 : k], "chan", n_chan, 2 * k) for k in range(1, n_chan // 2)]
    dw, gate = scatter_over_space(ids, dw, swap(dw_send, "chan", n_chan, 1), n_space)
    inv = after(inv, gate)

    dconv, dconv_send, edge, edge_send, sums = norm_backward(
        ids, count, dn, stand, inv, d_all[0], d_all[1], q, small, got)
    same_pairs, cross_pairs = [], []
    for s in range(n_space):
        for c in range(n_chan):
            t = s + 1 if c % 2 else s - 1
            if 0 <= t < n_space:
                same_pairs.append((s * n_chan + c, t * n_chan + c))
                cross_pairs.append((s * n_chan + c, t * n_chan + (c ^ 1)))
    same = lax.ppermute(edge, ("space", "chan"), same_pairs)
    cross = lax.ppermute(edge_send, ("space", "chan"), cross_pairs)
    other = swap(dconv_send, "chan", n_chan, 1)
    dw = sum(term.astype(F32) for term in dw) * grad_scale
    branch = after(branch, other)
    parts = [branch[0]] + [swap(branch[k], "chan", n_chan, k) for k in range(1, n_chan)]

    sums = kernel_grad(ids, dconv, other, image16, packed, sums)
    sums, sums_got = sum_over_space(sums, n_space)
    d_image = image_grad(ids, dconv, other, same, cross, cotangent, taps_back)
    output, d_kernel, d_shift, d_gain, d_scale, d_b_in = finish(ids, image, packed, sums, sums_got, parts)
    flat = [v.reshape(-1) for v in (d_gain, d_shift, d_b_in, d_scale)]
    return (output, d_image, d_kernel.T, *flat[:2], dw[0], flat[2], dw[1].T, flat[3])


def solution(mesh):
    return jax.shard_map(
        per_device,
        mesh=mesh,
        in_specs=(
            P("chan", ("groups", "space"), None),
            P("chan", None),
            P("chan"),
            P("chan"),
            P(None, "chan"),
            P("chan"),
            P("chan", None),
            P("chan"),
            P("chan", ("groups", "space"), None),
        ),
        out_specs=(
            P("chan", ("groups", "space"), None),
            P("chan", ("groups", "space"), None),
            P("chan", "groups"),
            P(("groups", "chan")),
            P(("groups", "chan")),
            P("space", ("groups", "chan")),
            P(("groups", "chan")),
            P(("groups", "chan"), "space"),
            P(("groups", "chan")),
        ),
        check_vma=False,
    )
```

```python
import functools

import jax
import jax.numpy as jnp
from jax import lax
from jax.experimental import pallas as pl
from jax.experimental.pallas import tpu as pltpu
from jax.sharding import PartitionSpec as P

BF = jnp.bfloat16
F32 = jnp.float32
grad_scale = 1.0 / 128.0
SLOTS = 16
VMEM = pl.BlockSpec(memory_space=pltpu.VMEM)
SMEM = pl.BlockSpec(memory_space=pltpu.SMEM)


def cost(microseconds):
    return pl.CostEstimate(flops=int(microseconds * 1.1e9), bytes_accessed=0, transcendentals=0)


def grant(mib):
    return pltpu.CompilerParams(vmem_limit_bytes=mib << 20)


HI = lax.Precision.HIGHEST
NT = (((1,), (1,)), ((), ()))


def column(row):
    return jnp.broadcast_to(row, (8, row.shape[1])).T[:, :1]


def shift_halves(a, b, by):
    if by == 0:
        return a, b
    lane = lax.broadcasted_iota(jnp.int32, a.shape, 1)
    k = (-by) % 128
    ra, rb = pltpu.roll(a, k, 1), pltpu.roll(b, k, 1)
    if by > 0:
        inner = lane < 128 - by
        return jnp.where(inner, ra, rb), jnp.where(inner, rb, 0.0)
    inner = lane >= -by
    return jnp.where(inner, ra, 0.0), jnp.where(inner, rb, ra)


def taps_kernel(flip, height, weight_ref, out_ref, rows_ref):
    local = out_ref.shape[0] // (7 * height)
    count = 7 * height
    tap = lax.broadcasted_iota(jnp.int32, (64, 128), 0)
    slot = lax.broadcasted_iota(jnp.int32, (64, 128), 1) % SLOTS
    row = jnp.where(slot < height + 3, slot, slot - SLOTS)
    weight = weight_ref[...].astype(F32).T[:local].astype(BF)
    for h in range(height):
        r = h + 3 - row if flip else row - h + 3
        base = jnp.where((r >= 0) & (r < 7) & (row >= -3), 7 * r, -100)
        for s in range(7):
            table = (tap == base + s).astype(F32).astype(BF)
            rows_ref[pl.ds((s * height + h) * local, local), :] = jnp.dot(
                weight, table, preferred_element_type=F32)
    lane = lax.broadcasted_iota(jnp.int32, (count, 128), 1) // SLOTS

    def body(g, carry):
        for u in range(0, 8, 2):
            pair = [
                jnp.where(lane == u + v, rows_ref[pl.ds(g * 8 + u + v, count, stride=local), :], 0.0)
                for v in range(2)
            ]
            start = pl.multiple_of((g * 8 + u) * count, 16)
            out_ref[pl.ds(start, 2 * count), :] = jnp.concatenate(pair, axis=0).astype(BF)
        return carry

    lax.fori_loop(0, local // 8, body, 0, unroll=6)


def make_taps(weight, local, height, flip):
    count = 7 * height
    return pl.pallas_call(
        functools.partial(taps_kernel, flip, height),
        out_shape=jax.ShapeDtypeStruct((local * count, 128), BF),
        in_specs=[VMEM],
        out_specs=VMEM,
        scratch_shapes=[pltpu.VMEM((count * local, 128), F32)],
        compiler_params=grant(6),
        cost_estimate=cost(2.4),
        name="taps_back" if flip else "taps_forward",
    )(weight)


def vector_of(lines, count):
    lines = lines.astype(F32)
    return [
        lines[r : r + 1] + lines[count + r : count + r + 1] + lines[2 * count + r : 2 * count + r + 1]
        for r in range(count)
    ]


def edge_kernel(ids_ref, image_ref, edge_a_ref, edge_b_ref, rows_ref):
    local, height, width = image_ref.shape
    odd = ids_ref[1] & 1

    def body(g, carry):
        for u in range(8):
            tile = image_ref[g * 8 + u].astype(F32)
            for part in range(2):
                rows_ref[part, pl.ds(g * 8 + u, height, stride=local), :] = tile[:, part * 128 : part * 128 + 128]
        return carry

    lax.fori_loop(0, local // 8, body, 0, unroll=6)
    top, bottom = (0, (height - 3) * local)
    for part in range(2):
        lanes = slice(part * 128, part * 128 + 128)
        to_a = pl.multiple_of(jnp.where(odd == 0, bottom, top), 16)
        to_b = pl.multiple_of(jnp.where(odd == 0, top, bottom), 16)
        edge_a_ref[:, lanes] = rows_ref[part, pl.ds(to_a, 3 * local), :].astype(BF)
        edge_b_ref[:, lanes] = rows_ref[part, pl.ds(to_b, 3 * local), :].astype(BF)


def edges(ids, image):
    local, height, width = image.shape
    return pl.pallas_call(
        edge_kernel,
        out_shape=[jax.ShapeDtypeStruct((3 * local, width), BF)] * 2,
        in_specs=[SMEM, VMEM],
        out_specs=[VMEM, VMEM],
        scratch_shapes=[pltpu.VMEM((2, height * local, 128), F32)],
        compiler_params=grant(3),
        cost_estimate=cost(1.2),
        name="edges",
    )(ids, image)


def pack_kernel(ids_ref, ct_ref, vector_ref, own_ref, send_ref, rows_ref, col_ref):
    local, height, width = ct_ref.shape
    core = ids_ref[0] & 1
    vector = vector_ref[...]
    count = vector.shape[1] // width
    col_ref[...] = column(vector)
    scale = col_ref[pl.ds(vector.shape[1] - 128, local), :]
    high = vector.astype(BF).astype(F32)
    middle = (vector - high).astype(BF).astype(F32)
    low = vector - high - middle
    lines = [part[:, r * width : r * width + width] for part in (high, middle, low) for r in range(count)]
    lines = jnp.concatenate(lines + [jnp.zeros((16 - 3 * count, width), F32)], axis=0).astype(BF)
    own_ref[pl.ds(height // 2 * local, 16), :] = lines
    send_ref[pl.ds(height // 2 * local, 16), :] = lines

    def body(g, carry):
        for u in range(8):
            tile = ct_ref[g * 8 + u].astype(F32)
            for part in range(2):
                rows_ref[part, pl.ds(g * 8 + u, height, stride=local), :] = tile[:, part * 128 : part * 128 + 128]
        return carry

    lax.fori_loop(0, local // 8, body, 0, unroll=6)
    for i in range(height // 2):
        rows = pl.ds(i * local, local)
        mine = pl.multiple_of((core * (height // 2) + i) * local, 16)
        theirs = pl.multiple_of(((1 - core) * (height // 2) + i) * local, 16)
        for part in range(2):
            lanes = slice(part * 128, part * 128 + 128)
            own_ref[rows, lanes] = (rows_ref[part, pl.ds(mine, local), :] * scale).astype(BF)
            send_ref[rows, lanes] = (rows_ref[part, pl.ds(theirs, local), :] * scale).astype(BF)


def pack(ids, ct, vector):
    local, height, width = ct.shape
    return pl.pallas_call(
        pack_kernel,
        out_shape=[jax.ShapeDtypeStruct((height // 2 * local + 16, width), BF)] * 2,
        in_specs=[SMEM, VMEM, VMEM],
        out_specs=[VMEM, VMEM],
        scratch_shapes=[
            pltpu.VMEM((2, height * local, 128), F32),
            pltpu.VMEM((vector.shape[1], 1), F32),
        ],
        compiler_params=grant(4),
        cost_estimate=cost(1.4),
        name="pack",
    )(ids, ct, vector)


def turn_kernel(*refs):
    for source, out in zip(refs[:4], refs[4:]):
        out[...] = source[...].T


def turn(*weights):
    return pl.pallas_call(
        turn_kernel,
        out_shape=[jax.ShapeDtypeStruct(w.shape[::-1], BF) for w in weights],
        in_specs=[VMEM] * 4,
        out_specs=[VMEM] * 4,
        compiler_params=grant(5),
        cost_estimate=cost(0.4),
        name="turn",
    )(*weights)


def merge_kernel(ids_ref, own_ref, got_ref, mine_ref, *rest):
    outs, buf = rest[:-1], rest[-1]
    rows = mine_ref.shape[1]
    me = ids_ref[1]
    for p in range(2):
        buf[...] = own_ref[p].astype(F32) + got_ref[p].astype(F32)
        mine_ref[p] = buf[pl.ds(pl.multiple_of(me * rows, 8), rows), :]
        for k, out in enumerate(outs):
            out[p] = buf[pl.ds(pl.multiple_of((me ^ (k + 1)) * rows, 8), rows), :].astype(BF)


def merge(ids, own, got, size):
    rows, hid = own.shape[1] // size, own.shape[2]
    return pl.pallas_call(
        merge_kernel,
        out_shape=[jax.ShapeDtypeStruct((2, rows, hid), F32)]
        + [jax.ShapeDtypeStruct((2, rows, hid), BF)] * (size - 1),
        in_specs=[SMEM, VMEM, VMEM],
        out_specs=[VMEM] * size,
        scratch_shapes=[pltpu.VMEM(own.shape[1:], F32)],
        compiler_params=grant(5),
        cost_estimate=cost(1),
        name="merge",
    )(ids, own, got)


def shift_sum(products, height, sign):
    left = products[3 * height : 4 * height, :128]
    right = products[3 * height : 4 * height, 128:]
    for s in (0, 1, 2, 4, 5, 6):
        block = products[s * height : (s + 1) * height]
        a, b = shift_halves(block[:, :128], block[:, 128:], sign * (s - 3))
        left, right = left + a, right + b
    return left, right


def conv_kernel(ids_ref, image_ref, got_a_ref, got_b_ref, taps_ref, own_ref, send_ref, image16_ref, acc_ref, rim_ref):
    local, height, width = image_ref.shape
    rows = own_ref.shape[0]
    count = 7 * height
    core, odd = ids_ref[0] & 1, ids_ref[1] & 1
    for part in range(2):
        lanes = slice(part * 128, part * 128 + 128)
        to_a = pl.multiple_of(5 * odd * local, 16)
        to_b = pl.multiple_of(5 * (1 - odd) * local, 16)
        rim_ref[part, pl.ds(to_a, 3 * local), :] = got_a_ref[:, lanes].astype(F32)
        rim_ref[part, pl.ds(to_b, 3 * local), :] = got_b_ref[:, lanes].astype(F32)
        rim_ref[part, pl.ds(3 * local, 2 * local), :] = jnp.zeros((2 * local, 128), F32)

    def body(g, carry):
        for u in range(8):
            ch = g * 8 + u
            pair = [rim_ref[p, pl.ds(ch, SLOTS - height, stride=local), :] for p in range(2)]
            tile = jnp.concatenate([image_ref[ch].astype(F32), jnp.concatenate(pair, axis=1)], axis=0)
            image16_ref[ch] = tile.astype(BF)
        right = image16_ref[pl.ds(g * 8, 8)].reshape(8 * SLOTS, width)
        taps = taps_ref[pl.ds(pl.multiple_of(g * 8 * count, 16), 8 * count), :]
        products = jnp.dot(taps, right, preferred_element_type=F32)
        for u in range(8):
            pair = shift_sum(products[u * count : (u + 1) * count], height, 1)
            for half in range(2):
                acc_ref[half, pl.ds(g * 8 + u, height, stride=local), :] = pair[half]
        return carry

    lax.fori_loop(0, local // 8, body, 0, unroll=6)
    for half in range(2):
        lanes = slice(half * 128, half * 128 + 128)
        mine = pl.multiple_of(core * rows, 16)
        theirs = pl.multiple_of((1 - core) * rows, 16)
        own_ref[:, lanes] = acc_ref[half, pl.ds(mine, rows), :].astype(BF)
        send_ref[:, lanes] = acc_ref[half, pl.ds(theirs, rows), :].astype(BF)


def conv_forward(ids, image, got_a, got_b, taps):
    local, height, width = image.shape
    rows = height // 2 * local
    return pl.pallas_call(
        conv_kernel,
        out_shape=[jax.ShapeDtypeStruct((rows, width), BF)] * 2
        + [jax.ShapeDtypeStruct((local, SLOTS, width), BF)],
        in_specs=[SMEM] + [VMEM] * 4,
        out_specs=[VMEM] * 3,
        scratch_shapes=[
            pltpu.VMEM((2, height * local, 128), F32),
            pltpu.VMEM((2, (SLOTS - height) * local, 128), F32),
        ],
        compiler_params=grant(6),
        cost_estimate=cost(5),
        name="conv_forward",
    )(ids, image, got_a, got_b, taps)


def mlp_kernel(blocks, count, me_ref, *refs):
    conv_refs = refs[:blocks]
    ct_refs = refs[blocks : 2 * blocks]
    (w_in_ref, w_inx_ref, w_int_ref, w_intx_ref, w_out_ref, w_outx_ref,
     w_outt_ref, w_outtx_ref) = refs[2 * blocks : 2 * blocks + 8]
    (branch_ref, dn_ref, dn_own_ref, stand_ref, inv_ref, q_ref, dw_ref, dwx_ref, small_ref,
     normed, dbranch, active, dhalf, centred, fold_ref, rounded, bias_ref, gain_ref, shift_ref,
     b_ref) = refs[2 * blocks + 8 :]
    me = me_ref[0]
    steps, _, width = inv_ref.shape
    hid = w_in_ref.shape[1]
    channels = w_in_ref.shape[0]
    local = channels // blocks

    def where(j):
        return pl.ds(pl.multiple_of((me ^ j) * local, 16), local)

    def chip(k):
        return pl.ds(pl.multiple_of(((me // 2) ^ k) * 2 * local, 16), 2 * local)

    def wide(value):
        return jnp.concatenate([value, value], axis=1)

    for j in range(blocks):
        lines = vector_of(ct_refs[j][pl.ds(steps * local, 16), :], count)
        cols = jnp.concatenate([column(line) for line in lines], axis=0)
        gain_ref[where(j), :] = jnp.broadcast_to(cols[:local], (local, 128))
        shift_ref[where(j), :] = jnp.broadcast_to(cols[local : 2 * local], (local, 128))
        if j < 2:
            b_ref[j] = jnp.broadcast_to(cols[2 * local : 2 * local + hid], (hid, 128))

    k0, k1 = (0.7978845608028654, 0.044715)
    parts = ((w_in_ref, w_int_ref, w_out_ref, w_outt_ref),
             (w_inx_ref, w_intx_ref, w_outx_ref, w_outtx_ref))
    for i in range(steps):
        rows = pl.ds(i * local, local)
        pixels = slice(i * width, i * width + width)
        for j in range(blocks):
            rounded[where(j), :] = conv_refs[j][rows, :]
            dbranch[where(j), pixels] = ct_refs[j][rows, :]
        value = rounded[...].astype(F32)
        average = jnp.sum(value, axis=0, keepdims=True) / channels
        value = value - average
        variance = jnp.sum(value * value, axis=0, keepdims=True) / channels
        inv_std = lax.rsqrt(variance + 1e-06)
        inv_ref[i] = inv_std
        stand = value * inv_std
        centred[...] = stand
        normed[:, pixels] = (stand * wide(gain_ref[...]) + wide(shift_ref[...])).astype(BF)
        stand_ref[pl.ds(i * 2 * local, 2 * local), :] = centred[chip(0), :]
        x = normed[:, pixels]
        d = dbranch[:, pixels]
        branch, dnormed = None, None
        for part, (w_in, w_int, w_out, w_outt) in enumerate(parts):
            pre = jnp.dot(w_int[...], x, preferred_element_type=F32) + wide(b_ref[part])
            dact = jnp.dot(w_out[...], d, preferred_element_type=F32)
            square = pre * pre
            th = jnp.tanh(pre * (k0 + (k0 * k1) * square))
            half = 0.5 * pre
            active[part, :, pixels] = (half + half * th).astype(BF)
            slope = 0.5 + 0.5 * th + half * (1.0 - th * th) * (k0 + (3.0 * k0 * k1) * square)
            dpre = dact * slope
            bias = dpre[:, :128] + dpre[:, 128:]
            bias_ref[part] = bias if i == 0 else bias_ref[part] + bias
            dhalf[part, :, pixels] = dpre.astype(BF)
            b_part = jnp.dot(w_outt[...], active[part, :, pixels], preferred_element_type=F32)
            d_part = jnp.dot(w_in[...], dhalf[part, :, pixels], preferred_element_type=F32)
            branch = b_part if part == 0 else branch + b_part
            dnormed = d_part if part == 0 else dnormed + d_part
        rounded[...] = branch.astype(BF)
        for j in range(blocks):
            branch_ref[j, rows, :] = rounded[where(j), :]
        scaled = dnormed * wide(gain_ref[...])
        first = jnp.sum(scaled, axis=0, keepdims=True)
        second = jnp.sum(scaled * centred[...], axis=0, keepdims=True)
        centred[...] = dnormed
        dn_own_ref[pl.ds(i * 2 * local, 2 * local), :] = centred[chip(0), :]
        q = jnp.concatenate([first, second], axis=0)
        q_ref[i] = q
        high = q.astype(BF).astype(F32)
        start = i * (2 * local + 16)
        extra = jnp.concatenate([high, q - high, jnp.zeros((12, width), F32)], axis=0).astype(BF)
        for k in range(1, blocks // 2):
            dn_ref[k - 1, pl.ds(start, 2 * local), :] = centred[chip(k), :].astype(BF)
            dn_ref[k - 1, pl.ds(start + 2 * local, 16), :] = extra

    ones = jnp.ones((8, 128), F32)

    def lane_sums(value):
        return lax.dot_general(ones, value, NT, preferred_element_type=F32, precision=HI)[:1]

    prod = None
    for part, out in ((0, dw_ref), (1, dwx_ref)):
        out[0] = lax.dot_general(normed[...], dhalf[part], NT, preferred_element_type=F32).astype(BF)
        d_out = lax.dot_general(dbranch[...], active[part], NT, preferred_element_type=F32)
        out[1] = d_out.astype(BF)
        term = d_out * parts[part][3][...].astype(F32)
        prod = term if part == 0 else prod + term
    if hid % 128:
        fold_ref[...] = jnp.concatenate(
            [jnp.sum(prod, axis=1, keepdims=True), jnp.zeros((channels, 127), F32)], axis=1)
    else:
        fold_ref[...] = sum(prod[:, i : i + 128] for i in range(128, hid, 128)) + prod[:, :128]
    pad = jnp.zeros((1, width - 2 * local), F32)
    for k in range(blocks // 2):
        line = jnp.concatenate([lane_sums(fold_ref[chip(k), :]), pad], axis=1)
        if k == 0:
            scale_line = line
        else:
            high = line.astype(BF).astype(F32)
            middle = (line - high).astype(BF).astype(F32)
            q = q_ref[steps - 1]
            q_high = q.astype(BF).astype(F32)
            extra = [q_high, q - q_high, high, middle, line - high - middle, jnp.zeros((9, width), F32)]
            dn_ref[k - 1, pl.ds(dn_ref.shape[1] - 16, 16), :] = jnp.concatenate(extra, axis=0).astype(BF)
    small_ref[0] = jnp.concatenate([scale_line, jnp.zeros((7, width), F32)], axis=0)
    for part in range(2):
        line = lane_sums(bias_ref[part])
        lines = [line[:, r * local : (r + 1) * local] for r in range(hid // local)]
        lines = jnp.concatenate(lines + [jnp.zeros((8 - len(lines), local), F32)], axis=0)
        small_ref[1 + part] = jnp.concatenate([lines, jnp.zeros((8, width - local), F32)], axis=1)


def mlp(me, conv, ct, count, weights):
    blocks = len(conv)
    rows, width = conv[0].shape
    channels, hid = weights[0].shape
    local = channels // blocks
    steps = rows // local
    peers = max(blocks // 2 - 1, 1)
    return pl.pallas_call(
        functools.partial(mlp_kernel, blocks, count),
        out_shape=[
            jax.ShapeDtypeStruct((blocks, rows, width), BF),
            jax.ShapeDtypeStruct((peers, steps * (2 * local + 16), width), BF),
            jax.ShapeDtypeStruct((2 * rows, width), F32),
            jax.ShapeDtypeStruct((2 * rows, width), F32),
            jax.ShapeDtypeStruct((steps, 1, width), F32),
            jax.ShapeDtypeStruct((steps, 2, width), F32),
            *[jax.ShapeDtypeStruct((2, channels, hid), BF)] * 2,
            jax.ShapeDtypeStruct((3, 8, width), F32),
        ],
        in_specs=[SMEM] + [VMEM] * (2 * blocks + 8),
        out_specs=[VMEM] * 9,
        scratch_shapes=[
            pltpu.VMEM((channels, rows // local * width), BF),
            pltpu.VMEM((channels, rows // local * width), BF),
            pltpu.VMEM((2, hid, rows // local * width), BF),
            pltpu.VMEM((2, hid, rows // local * width), BF),
            pltpu.VMEM((channels, width), F32),
            pltpu.VMEM((channels, 128), F32),
            pltpu.VMEM((channels, width), BF),
            pltpu.VMEM((2, hid, 128), F32),
            pltpu.VMEM((channels, 128), F32),
            pltpu.VMEM((channels, 128), F32),
            pltpu.VMEM((2, hid, 128), F32),
        ],
        compiler_params=grant(22),
        cost_estimate=cost(8),
        name="mlp",
    )(me, *conv, *ct, *weights)


def norm_kernel(peers, count, core_ref, *refs):
    dn_ref, stand_ref, inv_ref, vec_ref, vecx_ref, q_ref, small_ref = refs[:7]
    got = refs[7 : 7 + peers]
    (own_ref, send_ref, edge_own_ref, edge_send_ref, sums_ref, buf, gain_ref, fold_ref) = refs[7 + peers :]
    core = core_ref[0] & 1
    steps = inv_ref.shape[0]
    both = dn_ref.shape[0] // steps
    local = both // 2
    channels = both * (peers + 1)
    mine = pl.ds(pl.multiple_of(core * local, 16), local)
    theirs = pl.ds(pl.multiple_of((1 - core) * local, 16), local)
    last = pl.ds(vec_ref.shape[0] - 16, 16)
    gain_ref[mine, :] = column(vector_of(vec_ref[last, :], count)[0])[:local]
    gain_ref[theirs, :] = column(vector_of(vecx_ref[last, :], count)[0])[:local]
    shift_acc = jnp.zeros((both, 128), F32)
    gain_acc = jnp.zeros((both, 128), F32)
    for i in range(steps):
        rows = pl.ds(i * both, both)
        dn = dn_ref[rows, :]
        q = q_ref[i]
        for p in range(peers):
            start = i * (both + 16)
            dn = dn + got[p][0, pl.ds(start, both), :].astype(F32)
            extra = got[p][0, pl.ds(start + both, 16), :].astype(F32)
            q = q + (extra[0:2] + extra[2:4])
        q = q / channels
        stand = stand_ref[rows, :]
        prod = dn * stand
        shift_acc += dn[:, :128] + dn[:, 128:]
        gain_acc += prod[:, :128] + prod[:, 128:]
        buf[i] = inv_ref[i] * (dn * gain_ref[...] - q[0:1] - stand * q[1:2])
    for i in range(steps):
        own_ref[i] = buf[i, mine, :].astype(BF)
        send_ref[pl.ds(i * local, local), :] = buf[i, theirs, :].astype(BF)
    for i in range(3):
        edge_own_ref[i] = buf[i + core, mine, :].astype(BF)
        edge_send_ref[i] = buf[i + core, theirs, :].astype(BF)
    ones = jnp.ones((8, 128), F32)
    fold_ref[0], fold_ref[1] = shift_acc, gain_acc
    line = small_ref[0, pl.ds(0, 1), :]
    for p in range(peers):
        extra = got[p][0, pl.ds(got[p].shape[1] - 16, 16), :].astype(F32)
        line = line + (extra[4:5] + extra[5:6] + extra[6:7])
    low, high = line[:, :local], line[:, local : 2 * local]
    scale_mine = jnp.where(core == 0, low, high)
    scale_theirs = jnp.where(core == 0, high, low)
    for rows, scale, which in ((mine, scale_mine, 1), (theirs, scale_theirs, 2)):
        pair = [
            lax.dot_general(ones, fold_ref[k, rows, :], NT, preferred_element_type=F32, precision=HI)[:1]
            for k in range(2)
        ]
        bias = small_ref[which, pl.ds(0, 4), pl.ds(0, local)]
        sums = jnp.concatenate(pair + [scale, bias, jnp.zeros((1, local), F32)], axis=0)
        if which == 1:
            sums_ref[...] = sums
        else:
            high = sums.astype(BF).astype(F32)
            middle = (sums - high).astype(BF).astype(F32)
            lines = jnp.concatenate([high, middle, sums - high - middle, jnp.zeros((8, local), F32)], axis=0)
            width = send_ref.shape[1]
            lines = jnp.concatenate([lines, jnp.zeros((32, width - local), F32)], axis=1)
            send_ref[pl.ds(steps * local, 32), :] = lines.astype(BF)


def norm_backward(core, count, dn, stand, inv, vector, vector_x, q, small, got):
    steps, _, width = inv.shape
    both = dn.shape[0] // steps
    local = both // 2
    return pl.pallas_call(
        functools.partial(norm_kernel, len(got), count),
        out_shape=[
            jax.ShapeDtypeStruct((steps, local, width), BF),
            jax.ShapeDtypeStruct((steps * local + 32, width), BF),
            jax.ShapeDtypeStruct((3, local, width), BF),
            jax.ShapeDtypeStruct((3, local, width), BF),
            jax.ShapeDtypeStruct((8, local), F32),
        ],
        in_specs=[SMEM] + [VMEM] * (7 + len(got)),
        out_specs=[VMEM] * 5,
        scratch_shapes=[
            pltpu.VMEM((steps, both, width), F32),
            pltpu.VMEM((both, 1), F32),
            pltpu.VMEM((2, both, 128), F32),
        ],
        compiler_params=grant(5),
        cost_estimate=cost(1.3),
        name="norm_backward",
    )(core, dn, stand, inv, vector, vector_x, q, small, *got)


def fill_tile(rows_ref, own_ref, other_ref, core, local):
    half = own_ref.shape[0]
    for part in range(2):
        lanes = slice(part * 128, part * 128 + 128)
        for i in range(half):
            rows_ref[part, pl.ds(pl.multiple_of((core * half + i) * local, 8), local), :] = (
                own_ref[i, :, lanes].astype(F32))
            rows_ref[part, pl.ds(pl.multiple_of(((1 - core) * half + i) * local, 8), local), :] = (
                other_ref[pl.ds(i * local, local), lanes].astype(F32))


def kernel_grad_kernel(core_ref, own_ref, other_ref, image_ref, vector_ref, sums_ref, dkernel_ref, rows_ref,
                       corr_ref, line_ref):
    local, _, width = image_ref.shape
    height = 2 * own_ref.shape[0]
    count = 7 * height
    span = 16 * SLOTS
    fill_tile(rows_ref, own_ref, other_ref, core_ref[0] & 1, local)
    lane = lax.broadcasted_iota(jnp.int32, (count, span), 1) // SLOTS
    inner_slot = lax.broadcasted_iota(jnp.int32, (7, 128), 1) % SLOTS

    def body(g, carry):
        images = image_ref[pl.ds(g * 16, 16)].reshape(span, width)
        corr = jnp.zeros((count, span), F32)
        for first in range(0, 16, 8):
            stacks = []
            for inner in range(first, first + 8):
                a = rows_ref[0, pl.ds(g * 16 + inner, height, stride=local), :]
                b = rows_ref[1, pl.ds(g * 16 + inner, height, stride=local), :]
                stacks += [jnp.concatenate(shift_halves(a, b, 3 - s), axis=1) for s in range(7)]
            stack = jnp.concatenate(stacks, axis=0).astype(BF)
            value = lax.dot_general(stack, images, NT, preferred_element_type=F32)
            for inner in range(8):
                corr = jnp.where(lane == first + inner, value[inner * count : (inner + 1) * count], corr)
        for part in range(2):
            lanes = slice(part * 128, part * 128 + 128)
            corr_ref[part] = corr[:, lanes]
            line = corr_ref[part, pl.ds(0, 7, stride=height), :]
            for h in range(1, height):
                value = corr_ref[part, pl.ds(h, 7, stride=height), :]
                line = line + jnp.where(
                    inner_slot < SLOTS - h, pltpu.roll(value, 128 - h, 1), pltpu.roll(value, SLOTS - h, 1))
            line_ref[part, g, pl.ds(0, 7), :] = line
        return carry

    lax.fori_loop(0, local // 16, body, 0, unroll=3)
    slot = lax.broadcasted_iota(jnp.int32, (7, span), 1) % SLOTS
    total = jnp.zeros(dkernel_ref.shape, F32)
    for g in range(local // 16):
        lines = jnp.concatenate([line_ref[p, g, pl.ds(0, 7), :] for p in range(2)], axis=1)
        spread = [jnp.where(slot == (r - 3) % SLOTS, lines, 0.0) for r in range(7)] + [jnp.zeros((7, span), F32)]
        pick = (lax.broadcasted_iota(jnp.int32, (local, span), 0) - g * 16
                == lax.broadcasted_iota(jnp.int32, (local, span), 1) // SLOTS).astype(F32)
        total = total + lax.dot_general(
            jnp.concatenate(spread, axis=0), pick, NT, preferred_element_type=F32, precision=HI)
    dkernel_ref[...] = total * grad_scale
    lines = other_ref[pl.ds(height // 2 * local, 32), pl.ds(0, local)].astype(F32)
    sums = (sums_ref[...] + (lines[:8] + lines[8:16] + lines[16:24])) * grad_scale
    start = vector_ref.shape[1] - 128
    scale_line = sums[2:3] / vector_ref[:, start : start + local]
    dkernel_ref[pl.ds(49, 7), :] = jnp.concatenate([sums[:2], scale_line, sums[3:7]], axis=0)


def kernel_grad(core, own, other, image16, vector, sums):
    local = image16.shape[0]
    height = 2 * own.shape[0]
    return pl.pallas_call(
        kernel_grad_kernel,
        out_shape=jax.ShapeDtypeStruct((56, local), F32),
        in_specs=[SMEM] + [VMEM] * 5,
        out_specs=VMEM,
        scratch_shapes=[
            pltpu.VMEM((2, height * local, 128), F32),
            pltpu.VMEM((2, 7 * height, 128), F32),
            pltpu.VMEM((2, local // 16, 8, 128), F32),
        ],
        compiler_params=grant(5),
        cost_estimate=cost(4),
        name="kernel_grad",
    )(core, own, other, image16, vector, sums)


def image_grad_kernel(core_ref, own_ref, other_ref, same_ref, cross_ref, ct_ref, taps_ref, out_ref, rows_ref):
    local, height, width = ct_ref.shape
    core = core_ref[0] & 1
    count = 7 * height
    fill_tile(rows_ref, own_ref, other_ref, core, local)
    for part in range(2):
        lanes = slice(part * 128, part * 128 + 128)
        for i in range(3):
            a = pl.multiple_of((height + 5 * core + i) * local, 8)
            b = pl.multiple_of((height + 5 * (1 - core) + i) * local, 8)
            rows_ref[part, pl.ds(a, local), :] = same_ref[i, :, lanes].astype(F32)
            rows_ref[part, pl.ds(b, local), :] = cross_ref[i, :, lanes].astype(F32)
        rows_ref[part, pl.ds((height + 3) * local, 2 * local), :] = jnp.zeros((2 * local, 128), F32)

    def body(g, carry):
        tiles = []
        for u in range(8):
            pair = [rows_ref[p, pl.ds(g * 8 + u, SLOTS, stride=local), :] for p in range(2)]
            tiles.append(jnp.concatenate(pair, axis=1))
        right = jnp.concatenate(tiles, axis=0).astype(BF)
        start = pl.multiple_of(g * 8 * count, 16)
        products = jnp.dot(taps_ref[pl.ds(start, 8 * count), :], right, preferred_element_type=F32)
        for u in range(8):
            ch = g * 8 + u
            left_right = shift_sum(products[u * count : (u + 1) * count], height, -1)
            out_ref[ch] = (ct_ref[ch].astype(F32) + jnp.concatenate(left_right, axis=1)).astype(BF)
        return carry

    lax.fori_loop(0, local // 8, body, 0, unroll=6)


def image_grad(core, own, other, same, cross, ct, taps):
    local, height, width = ct.shape
    return pl.pallas_call(
        image_grad_kernel,
        out_shape=jax.ShapeDtypeStruct((local, height, width), BF),
        in_specs=[SMEM] + [VMEM] * 6,
        out_specs=VMEM,
        scratch_shapes=[pltpu.VMEM((2, SLOTS * local, 128), F32)],
        compiler_params=grant(6),
        cost_estimate=cost(5),
        name="image_grad",
    )(core, own, other, same, cross, ct, taps)


def finish_kernel(blocks, core_ref, image_ref, vector_ref, *refs):
    part_refs = refs[:blocks]
    out_ref, rows_ref, col_ref = refs[blocks:]
    local, height, width = image_ref.shape
    half = height // 2
    core = core_ref[0] & 1
    col_ref[...] = column(vector_ref[...])
    scale = col_ref[pl.ds(vector_ref.shape[1] - 128, local), :]
    for which in range(2):
        place = core if which == 0 else 1 - core
        for i in range(half):
            rows = pl.ds(i * local, local)
            total = part_refs[which][rows, :].astype(F32)
            for k in range(which + 2, blocks, 2):
                total = total + part_refs[k][rows, :].astype(F32)
            total = total * scale
            start = pl.multiple_of((place * half + i) * local, 8)
            for part in range(2):
                rows_ref[part, pl.ds(start, local), :] = total[:, part * 128 : part * 128 + 128]

    def body(g, carry):
        for u in range(8):
            ch = g * 8 + u
            pair = [rows_ref[p, pl.ds(ch, height, stride=local), :] for p in range(2)]
            out_ref[ch] = (image_ref[ch].astype(F32) + jnp.concatenate(pair, axis=1)).astype(BF)
        return carry

    lax.fori_loop(0, local // 8, body, 0, unroll=6)


def finish(core, image, vector, parts):
    local, height, width = image.shape
    return pl.pallas_call(
        functools.partial(finish_kernel, len(parts)),
        out_shape=jax.ShapeDtypeStruct((local, height, width), BF),
        in_specs=[SMEM] + [VMEM] * (2 + len(parts)),
        out_specs=VMEM,
        scratch_shapes=[
            pltpu.VMEM((2, height * local, 128), F32),
            pltpu.VMEM((vector.shape[1], 1), F32),
        ],
        compiler_params=grant(5),
        cost_estimate=cost(2),
        name="finish",
    )(core, image, vector, *parts)


def totals_kernel(sums_ref, sums_got_ref, dkernel_ref, shift_ref, gain_ref, scale_ref, bias_ref):
    sums = sums_ref[...] + sums_got_ref[...]
    dkernel_ref[...] = sums[:49]
    shift_ref[...], gain_ref[...], scale_ref[...] = sums[49:50], sums[50:51], sums[51:52]
    bias = jnp.concatenate([sums[52 + i : 53 + i] for i in range(4)], axis=1)
    lanes = bias_ref.shape[1]
    bias_ref[...] = jnp.concatenate(
        [bias[:, i * lanes : (i + 1) * lanes] for i in range(bias_ref.shape[0])], axis=0)


def totals(sums, sums_got):
    local = sums.shape[1]
    return pl.pallas_call(
        totals_kernel,
        out_shape=[
            jax.ShapeDtypeStruct((49, local), F32),
            *[jax.ShapeDtypeStruct((1, local), F32)] * 3,
            jax.ShapeDtypeStruct((local // 32, 128) if local % 32 == 0 else (1, 4 * local), F32),
        ],
        in_specs=[VMEM, VMEM],
        out_specs=[VMEM] * 5,
        compiler_params=grant(2),
        cost_estimate=cost(0.4),
        name="totals",
    )(sums, sums_got)


def swap(value, axis, size, k):
    return lax.ppermute(value, axis, [(i, i ^ k) for i in range(size)])


def after(value, *gates):
    return lax.optimization_barrier((value, *gates))[0]


def sum_over_space(value, size):
    k = 1
    while 2 * k < size:
        value = value + swap(value, "space", size, k)
        k *= 2
    return value, k


def scatter_over_space(ids, own, got, size):
    if size > 4:
        total = (own.astype(F32) + got.astype(F32)).astype(BF)
        return [lax.psum_scatter(total, "space", scatter_dimension=1, tiled=True)], total
    mine, *others = merge(ids, own, got, size)
    return [mine] + [swap(p, "space", size, k + 1) for k, p in enumerate(others)], mine


def per_device(image, dw_weight, ln_gain, ln_shift, w_in, b_in, w_out, layer_scale, cotangent):
    local, height, width = image.shape
    hid = w_in.shape[1]
    n_chan, n_space = lax.axis_size("chan"), lax.axis_size("space")
    ids = jnp.stack([lax.axis_index("chan"), lax.axis_index("space")]).astype(jnp.int32)

    used = 2 * local + hid + 128
    count = -(-used // width)
    parts = [ln_gain, ln_shift, b_in, jnp.zeros(count * width - used, F32), layer_scale, jnp.zeros(128 - local, F32)]
    packed = jnp.concatenate([v for v in parts if v.size])[None]
    d_mine, d_theirs = pack(ids, cotangent, packed)
    d_all = [d_mine] + [
        swap(d_theirs if k % 2 else d_mine, "chan", n_chan, k) for k in range(1, n_chan)
    ]
    pairs_a = [(s, s ^ 1) for s in range(n_space) if s ^ 1 < n_space]
    pairs_b = [(s, t) for s in range(n_space) for t in [s + 1 if s % 2 else s - 1] if 0 <= t < n_space]
    edge_a, edge_b = edges(ids, after(image, d_mine))
    got_a = lax.ppermute(edge_a, "space", pairs_a)
    got_b = lax.ppermute(edge_b, "space", pairs_b)
    dw_weight, w_in, w_out = lax.optimization_barrier((dw_weight, w_in, w_out, edge_a))[:3]
    w_inx = swap(w_in, "chan", n_chan, 1)
    w_outx = swap(w_out, "chan", n_chan, 1)
    weight = jnp.pad(dw_weight.T, ((0, 15), (0, -local % 128)))
    taps = make_taps(weight, local, height, False)
    taps, d_all = lax.optimization_barrier((taps, d_all))

    mine, theirs, image16 = conv_forward(ids, image, got_a, got_b, taps)
    conv = [mine] + [swap(theirs if k % 2 else mine, "chan", n_chan, k) for k in range(1, n_chan)]
    w_in, w_inx, w_out, w_outx, weight = lax.optimization_barrier((w_in, w_inx, w_out, w_outx, weight, mine))[:5]
    w_int, w_intx, w_outt, w_outtx = turn(w_in, w_inx, w_out, w_outx)
    taps_back = make_taps(weight, local, height, True)
    weights = [w_in, w_inx, w_int, w_intx, w_out, w_outx, w_outt, w_outtx]
    conv[0] = after(conv[0], taps_back)
    branch, dn_send, dn, stand, inv, q, dw, dw_send, small = mlp(ids, conv, d_all, count, weights)

    got = [swap(dn_send[k - 1 : k], "chan", n_chan, 2 * k) for k in range(1, n_chan // 2)]
    dw, gate = scatter_over_space(ids, dw, swap(dw_send, "chan", n_chan, 1), n_space)
    inv = after(inv, gate)

    dconv, dconv_send, edge, edge_send, sums = norm_backward(
        ids, count, dn, stand, inv, d_all[0], d_all[1], q, small, got)
    same_pairs, cross_pairs = [], []
    for s in range(n_space):
        for c in range(n_chan):
            t = s + 1 if c % 2 else s - 1
            if 0 <= t < n_space:
                same_pairs.append((s * n_chan + c, t * n_chan + c))
                cross_pairs.append((s * n_chan + c, t * n_chan + (c ^ 1)))
    same = lax.ppermute(edge, ("space", "chan"), same_pairs)
    cross = lax.ppermute(edge_send, ("space", "chan"), cross_pairs)
    other = swap(dconv_send, "chan", n_chan, 1)
    dw = sum(term.astype(F32) for term in dw) * grad_scale
    branch = after(branch, other)
    parts = [branch[0]] + [swap(branch[k], "chan", n_chan, k) for k in range(1, n_chan)]

    sums = kernel_grad(ids, dconv, other, image16, packed, after(sums, parts[1]))
    sums, last = sum_over_space(sums, n_space)
    d_image = image_grad(ids, dconv, other, same, cross, cotangent, taps_back)
    sums = after(sums, d_image)
    sums_got = swap(sums, "space", n_space, last)
    output = finish(ids, image, packed, parts)
    d_kernel, d_shift, d_gain, d_scale, d_b_in = totals(sums, sums_got)
    flat = [v.reshape(-1) for v in (d_gain, d_shift, d_b_in, d_scale)]
    return (output, d_image, d_kernel.T, *flat[:2], dw[0], flat[2], dw[1].T, flat[3])


def solution(mesh):
    return jax.shard_map(
        per_device,
        mesh=mesh,
        in_specs=(
            P("chan", ("groups", "space"), None),
            P("chan", None),
            P("chan"),
            P("chan"),
            P(None, "chan"),
            P("chan"),
            P("chan", None),
            P("chan"),
            P("chan", ("groups", "space"), None),
        ),
        out_specs=(
            P("chan", ("groups", "space"), None),
            P("chan", ("groups", "space"), None),
            P("chan", "groups"),
            P(("groups", "chan")),
            P(("groups", "chan")),
            P("space", ("groups", "chan")),
            P(("groups", "chan")),
            P(("groups", "chan"), "space"),
            P(("groups", "chan")),
        ),
        check_vma=False,
    )
```

```python
import functools

import jax
import jax.numpy as jnp
from jax import lax
from jax.experimental import pallas as pl
from jax.experimental.pallas import tpu as pltpu
from jax.sharding import PartitionSpec as P

BF = jnp.bfloat16
F32 = jnp.float32
grad_scale = 1.0 / 128.0
SLOTS = 16
VMEM = pl.BlockSpec(memory_space=pltpu.VMEM)
SMEM = pl.BlockSpec(memory_space=pltpu.SMEM)


def cost(microseconds):
    return pl.CostEstimate(flops=int(microseconds * 1.1e9), bytes_accessed=0, transcendentals=0)


def grant(mib):
    return pltpu.CompilerParams(vmem_limit_bytes=mib << 20)


HI = lax.Precision.HIGHEST
NT = (((1,), (1,)), ((), ()))


def column(row):
    return jnp.broadcast_to(row, (8, row.shape[1])).T[:, :1]


def shift_halves(a, b, by):
    if by == 0:
        return a, b
    lane = lax.broadcasted_iota(jnp.int32, a.shape, 1)
    k = (-by) % 128
    ra, rb = pltpu.roll(a, k, 1), pltpu.roll(b, k, 1)
    if by > 0:
        inner = lane < 128 - by
        return jnp.where(inner, ra, rb), jnp.where(inner, rb, 0.0)
    inner = lane >= -by
    return jnp.where(inner, ra, 0.0), jnp.where(inner, rb, ra)


def taps_kernel(flip, height, weight_ref, out_ref, rows_ref):
    local = out_ref.shape[0] // (7 * height)
    count = 7 * height
    tap = lax.broadcasted_iota(jnp.int32, (64, 128), 0)
    slot = lax.broadcasted_iota(jnp.int32, (64, 128), 1) % SLOTS
    row = jnp.where(slot < height + 3, slot, slot - SLOTS)
    weight = weight_ref[...].astype(F32).T[:local].astype(BF)
    for h in range(height):
        r = h + 3 - row if flip else row - h + 3
        base = jnp.where((r >= 0) & (r < 7) & (row >= -3), 7 * r, -100)
        for s in range(7):
            table = (tap == base + s).astype(F32).astype(BF)
            rows_ref[pl.ds((s * height + h) * local, local), :] = jnp.dot(
                weight, table, preferred_element_type=F32)
    lane = lax.broadcasted_iota(jnp.int32, (count, 128), 1) // SLOTS

    def body(g, carry):
        for u in range(0, 8, 2):
            pair = [
                jnp.where(lane == u + v, rows_ref[pl.ds(g * 8 + u + v, count, stride=local), :], 0.0)
                for v in range(2)
            ]
            start = pl.multiple_of((g * 8 + u) * count, 16)
            out_ref[pl.ds(start, 2 * count), :] = jnp.concatenate(pair, axis=0).astype(BF)
        return carry

    lax.fori_loop(0, local // 8, body, 0, unroll=6)


def make_taps(weight, local, height, flip):
    count = 7 * height
    return pl.pallas_call(
        functools.partial(taps_kernel, flip, height),
        out_shape=jax.ShapeDtypeStruct((local * count, 128), BF),
        in_specs=[VMEM],
        out_specs=VMEM,
        scratch_shapes=[pltpu.VMEM((count * local, 128), F32)],
        compiler_params=grant(6),
        cost_estimate=cost(2.4),
        name="taps_back" if flip else "taps_forward",
    )(weight)


def vector_of(lines, count):
    lines = lines.astype(F32)
    return [
        lines[r : r + 1] + lines[count + r : count + r + 1] + lines[2 * count + r : 2 * count + r + 1]
        for r in range(count)
    ]


def edge_kernel(ids_ref, image_ref, edge_a_ref, edge_b_ref, rows_ref):
    local, height, width = image_ref.shape
    odd = ids_ref[1] & 1

    def body(g, carry):
        for u in range(8):
            tile = image_ref[g * 8 + u].astype(F32)
            for part in range(2):
                rows_ref[part, pl.ds(g * 8 + u, height, stride=local), :] = tile[:, part * 128 : part * 128 + 128]
        return carry

    lax.fori_loop(0, local // 8, body, 0, unroll=6)
    top, bottom = (0, (height - 3) * local)
    for part in range(2):
        lanes = slice(part * 128, part * 128 + 128)
        to_a = pl.multiple_of(jnp.where(odd == 0, bottom, top), 16)
        to_b = pl.multiple_of(jnp.where(odd == 0, top, bottom), 16)
        edge_a_ref[:, lanes] = rows_ref[part, pl.ds(to_a, 3 * local), :].astype(BF)
        edge_b_ref[:, lanes] = rows_ref[part, pl.ds(to_b, 3 * local), :].astype(BF)


def edges(ids, image):
    local, height, width = image.shape
    return pl.pallas_call(
        edge_kernel,
        out_shape=[jax.ShapeDtypeStruct((3 * local, width), BF)] * 2,
        in_specs=[SMEM, VMEM],
        out_specs=[VMEM, VMEM],
        scratch_shapes=[pltpu.VMEM((2, height * local, 128), F32)],
        compiler_params=grant(3),
        cost_estimate=cost(1.2),
        name="edges",
    )(ids, image)


def pack_kernel(ids_ref, ct_ref, vector_ref, own_ref, send_ref, rows_ref, col_ref):
    local, height, width = ct_ref.shape
    core = ids_ref[0] & 1
    vector = vector_ref[...]
    count = vector.shape[1] // width
    col_ref[...] = column(vector)
    scale = col_ref[pl.ds(vector.shape[1] - 128, local), :]
    high = vector.astype(BF).astype(F32)
    middle = (vector - high).astype(BF).astype(F32)
    low = vector - high - middle
    lines = [part[:, r * width : r * width + width] for part in (high, middle, low) for r in range(count)]
    lines = jnp.concatenate(lines + [jnp.zeros((16 - 3 * count, width), F32)], axis=0).astype(BF)
    own_ref[pl.ds(height // 2 * local, 16), :] = lines
    send_ref[pl.ds(height // 2 * local, 16), :] = lines

    def body(g, carry):
        for u in range(8):
            tile = ct_ref[g * 8 + u].astype(F32)
            for part in range(2):
                rows_ref[part, pl.ds(g * 8 + u, height, stride=local), :] = tile[:, part * 128 : part * 128 + 128]
        return carry

    lax.fori_loop(0, local // 8, body, 0, unroll=6)
    for i in range(height // 2):
        rows = pl.ds(i * local, local)
        mine = pl.multiple_of((core * (height // 2) + i) * local, 16)
        theirs = pl.multiple_of(((1 - core) * (height // 2) + i) * local, 16)
        for part in range(2):
            lanes = slice(part * 128, part * 128 + 128)
            own_ref[rows, lanes] = (rows_ref[part, pl.ds(mine, local), :] * scale).astype(BF)
            send_ref[rows, lanes] = (rows_ref[part, pl.ds(theirs, local), :] * scale).astype(BF)


def pack(ids, ct, vector):
    local, height, width = ct.shape
    return pl.pallas_call(
        pack_kernel,
        out_shape=[jax.ShapeDtypeStruct((height // 2 * local + 16, width), BF)] * 2,
        in_specs=[SMEM, VMEM, VMEM],
        out_specs=[VMEM, VMEM],
        scratch_shapes=[
            pltpu.VMEM((2, height * local, 128), F32),
            pltpu.VMEM((vector.shape[1], 1), F32),
        ],
        compiler_params=grant(4),
        cost_estimate=cost(1.4),
        name="pack",
    )(ids, ct, vector)


def turn_kernel(*refs):
    for source, out in zip(refs[:4], refs[4:]):
        out[...] = source[...].T


def turn(*weights):
    return pl.pallas_call(
        turn_kernel,
        out_shape=[jax.ShapeDtypeStruct(w.shape[::-1], BF) for w in weights],
        in_specs=[VMEM] * 4,
        out_specs=[VMEM] * 4,
        compiler_params=grant(5),
        cost_estimate=cost(0.4),
        name="turn",
    )(*weights)


def merge_kernel(ids_ref, own_ref, got_ref, mine_ref, *rest):
    outs, buf = rest[:-1], rest[-1]
    rows = mine_ref.shape[1]
    me = ids_ref[1]
    for p in range(2):
        buf[...] = own_ref[p].astype(F32) + got_ref[p].astype(F32)
        mine_ref[p] = buf[pl.ds(pl.multiple_of(me * rows, 8), rows), :]
        for k, out in enumerate(outs):
            out[p] = buf[pl.ds(pl.multiple_of((me ^ (k + 1)) * rows, 8), rows), :].astype(BF)


def merge(ids, own, got, size):
    rows, hid = own.shape[1] // size, own.shape[2]
    return pl.pallas_call(
        merge_kernel,
        out_shape=[jax.ShapeDtypeStruct((2, rows, hid), F32)]
        + [jax.ShapeDtypeStruct((2, rows, hid), BF)] * (size - 1),
        in_specs=[SMEM, VMEM, VMEM],
        out_specs=[VMEM] * size,
        scratch_shapes=[pltpu.VMEM(own.shape[1:], F32)],
        compiler_params=grant(5),
        cost_estimate=cost(1),
        name="merge",
    )(ids, own, got)


def shift_sum(products, height, sign):
    left = products[3 * height : 4 * height, :128]
    right = products[3 * height : 4 * height, 128:]
    for s in (0, 1, 2, 4, 5, 6):
        block = products[s * height : (s + 1) * height]
        a, b = shift_halves(block[:, :128], block[:, 128:], sign * (s - 3))
        left, right = left + a, right + b
    return left, right


def conv_kernel(ids_ref, image_ref, got_a_ref, got_b_ref, taps_ref, own_ref, send_ref, image16_ref, acc_ref, rim_ref):
    local, height, width = image_ref.shape
    rows = own_ref.shape[0]
    count = 7 * height
    core, odd = ids_ref[0] & 1, ids_ref[1] & 1
    for part in range(2):
        lanes = slice(part * 128, part * 128 + 128)
        to_a = pl.multiple_of(5 * odd * local, 16)
        to_b = pl.multiple_of(5 * (1 - odd) * local, 16)
        rim_ref[part, pl.ds(to_a, 3 * local), :] = got_a_ref[:, lanes].astype(F32)
        rim_ref[part, pl.ds(to_b, 3 * local), :] = got_b_ref[:, lanes].astype(F32)
        rim_ref[part, pl.ds(3 * local, 2 * local), :] = jnp.zeros((2 * local, 128), F32)

    def body(g, carry):
        for u in range(8):
            ch = g * 8 + u
            pair = [rim_ref[p, pl.ds(ch, SLOTS - height, stride=local), :] for p in range(2)]
            tile = jnp.concatenate([image_ref[ch].astype(F32), jnp.concatenate(pair, axis=1)], axis=0)
            image16_ref[ch] = tile.astype(BF)
        right = image16_ref[pl.ds(g * 8, 8)].reshape(8 * SLOTS, width)
        taps = taps_ref[pl.ds(pl.multiple_of(g * 8 * count, 16), 8 * count), :]
        products = jnp.dot(taps, right, preferred_element_type=F32)
        for u in range(8):
            pair = shift_sum(products[u * count : (u + 1) * count], height, 1)
            for half in range(2):
                acc_ref[half, pl.ds(g * 8 + u, height, stride=local), :] = pair[half]
        return carry

    lax.fori_loop(0, local // 8, body, 0, unroll=True)
    for half in range(2):
        lanes = slice(half * 128, half * 128 + 128)
        mine = pl.multiple_of(core * rows, 16)
        theirs = pl.multiple_of((1 - core) * rows, 16)
        own_ref[:, lanes] = acc_ref[half, pl.ds(mine, rows), :].astype(BF)
        send_ref[:, lanes] = acc_ref[half, pl.ds(theirs, rows), :].astype(BF)


def conv_forward(ids, image, got_a, got_b, taps):
    local, height, width = image.shape
    rows = height // 2 * local
    return pl.pallas_call(
        conv_kernel,
        out_shape=[jax.ShapeDtypeStruct((rows, width), BF)] * 2
        + [jax.ShapeDtypeStruct((local, SLOTS, width), BF)],
        in_specs=[SMEM] + [VMEM] * 4,
        out_specs=[VMEM] * 3,
        scratch_shapes=[
            pltpu.VMEM((2, height * local, 128), F32),
            pltpu.VMEM((2, (SLOTS - height) * local, 128), F32),
        ],
        compiler_params=grant(6),
        cost_estimate=cost(5),
        name="conv_forward",
    )(ids, image, got_a, got_b, taps)


def mlp_kernel(blocks, count, me_ref, *refs):
    conv_refs = refs[:blocks]
    ct_refs = refs[blocks : 2 * blocks]
    (w_in_ref, w_inx_ref, w_int_ref, w_intx_ref, w_out_ref, w_outx_ref,
     w_outt_ref, w_outtx_ref) = refs[2 * blocks : 2 * blocks + 8]
    (branch_ref, dn_ref, dn_own_ref, stand_ref, inv_ref, q_ref, dw_ref, dwx_ref, small_ref,
     normed, dbranch, active, dhalf, centred, fold_ref, rounded, bias_ref, gain_ref, shift_ref,
     b_ref) = refs[2 * blocks + 8 :]
    me = me_ref[0]
    steps, _, width = inv_ref.shape
    hid = w_in_ref.shape[1]
    channels = w_in_ref.shape[0]
    local = channels // blocks

    def where(j):
        return pl.ds(pl.multiple_of((me ^ j) * local, 16), local)

    def chip(k):
        return pl.ds(pl.multiple_of(((me // 2) ^ k) * 2 * local, 16), 2 * local)

    def wide(value):
        return jnp.concatenate([value, value], axis=1)

    for j in range(blocks):
        lines = vector_of(ct_refs[j][pl.ds(steps * local, 16), :], count)
        cols = jnp.concatenate([column(line) for line in lines], axis=0)
        gain_ref[where(j), :] = jnp.broadcast_to(cols[:local], (local, 128))
        shift_ref[where(j), :] = jnp.broadcast_to(cols[local : 2 * local], (local, 128))
        if j < 2:
            b_ref[j] = jnp.broadcast_to(cols[2 * local : 2 * local + hid], (hid, 128))

    k0, k1 = (0.7978845608028654, 0.044715)
    parts = ((w_in_ref, w_int_ref, w_out_ref, w_outt_ref),
             (w_inx_ref, w_intx_ref, w_outx_ref, w_outtx_ref))
    for i in range(steps):
        rows = pl.ds(i * local, local)
        pixels = slice(i * width, i * width + width)
        for j in range(blocks):
            rounded[where(j), :] = conv_refs[j][rows, :]
            dbranch[where(j), pixels] = ct_refs[j][rows, :]
        value = rounded[...].astype(F32)
        average = jnp.sum(value, axis=0, keepdims=True) / channels
        value = value - average
        variance = jnp.sum(value * value, axis=0, keepdims=True) / channels
        inv_std = lax.rsqrt(variance + 1e-06)
        inv_ref[i] = inv_std
        stand = value * inv_std
        centred[...] = stand
        normed[:, pixels] = (stand * wide(gain_ref[...]) + wide(shift_ref[...])).astype(BF)
        stand_ref[pl.ds(i * 2 * local, 2 * local), :] = centred[chip(0), :]
        x = normed[:, pixels]
        d = dbranch[:, pixels]
        branch, dnormed = None, None
        for part, (w_in, w_int, w_out, w_outt) in enumerate(parts):
            pre = jnp.dot(w_int[...], x, preferred_element_type=F32) + wide(b_ref[part])
            dact = jnp.dot(w_out[...], d, preferred_element_type=F32)
            square = pre * pre
            th = jnp.tanh(pre * (k0 + (k0 * k1) * square))
            half = 0.5 * pre
            active[part, :, pixels] = (half + half * th).astype(BF)
            slope = 0.5 + 0.5 * th + half * (1.0 - th * th) * (k0 + (3.0 * k0 * k1) * square)
            dpre = dact * slope
            bias = dpre[:, :128] + dpre[:, 128:]
            bias_ref[part] = bias if i == 0 else bias_ref[part] + bias
            dhalf[part, :, pixels] = dpre.astype(BF)
            b_part = jnp.dot(w_outt[...], active[part, :, pixels], preferred_element_type=F32)
            d_part = jnp.dot(w_in[...], dhalf[part, :, pixels], preferred_element_type=F32)
            branch = b_part if part == 0 else branch + b_part
            dnormed = d_part if part == 0 else dnormed + d_part
        rounded[...] = branch.astype(BF)
        for j in range(blocks):
            branch_ref[j, rows, :] = rounded[where(j), :]
        scaled = dnormed * wide(gain_ref[...])
        first = jnp.sum(scaled, axis=0, keepdims=True)
        second = jnp.sum(scaled * centred[...], axis=0, keepdims=True)
        centred[...] = dnormed
        dn_own_ref[pl.ds(i * 2 * local, 2 * local), :] = centred[chip(0), :]
        q = jnp.concatenate([first, second], axis=0)
        q_ref[i] = q
        high = q.astype(BF).astype(F32)
        start = i * (2 * local + 16)
        extra = jnp.concatenate([high, q - high, jnp.zeros((12, width), F32)], axis=0).astype(BF)
        for k in range(1, blocks // 2):
            dn_ref[k - 1, pl.ds(start, 2 * local), :] = centred[chip(k), :].astype(BF)
            dn_ref[k - 1, pl.ds(start + 2 * local, 16), :] = extra

    ones = jnp.ones((8, 128), F32)

    def lane_sums(value):
        return lax.dot_general(ones, value, NT, preferred_element_type=F32, precision=HI)[:1]

    prod = None
    for part, out in ((0, dw_ref), (1, dwx_ref)):
        out[0] = lax.dot_general(normed[...], dhalf[part], NT, preferred_element_type=F32).astype(BF)
        d_out = lax.dot_general(dbranch[...], active[part], NT, preferred_element_type=F32)
        out[1] = d_out.astype(BF)
        term = d_out * parts[part][3][...].astype(F32)
        prod = term if part == 0 else prod + term
    if hid % 128:
        fold_ref[...] = jnp.concatenate(
            [jnp.sum(prod, axis=1, keepdims=True), jnp.zeros((channels, 127), F32)], axis=1)
    else:
        fold_ref[...] = sum(prod[:, i : i + 128] for i in range(128, hid, 128)) + prod[:, :128]
    pad = jnp.zeros((1, width - 2 * local), F32)
    for k in range(blocks // 2):
        line = jnp.concatenate([lane_sums(fold_ref[chip(k), :]), pad], axis=1)
        if k == 0:
            scale_line = line
        else:
            high = line.astype(BF).astype(F32)
            middle = (line - high).astype(BF).astype(F32)
            q = q_ref[steps - 1]
            q_high = q.astype(BF).astype(F32)
            extra = [q_high, q - q_high, high, middle, line - high - middle, jnp.zeros((9, width), F32)]
            dn_ref[k - 1, pl.ds(dn_ref.shape[1] - 16, 16), :] = jnp.concatenate(extra, axis=0).astype(BF)
    small_ref[0] = jnp.concatenate([scale_line, jnp.zeros((7, width), F32)], axis=0)
    for part in range(2):
        line = lane_sums(bias_ref[part])
        lines = [line[:, r * local : (r + 1) * local] for r in range(hid // local)]
        lines = jnp.concatenate(lines + [jnp.zeros((8 - len(lines), local), F32)], axis=0)
        small_ref[1 + part] = jnp.concatenate([lines, jnp.zeros((8, width - local), F32)], axis=1)


def mlp(me, conv, ct, count, weights):
    blocks = len(conv)
    rows, width = conv[0].shape
    channels, hid = weights[0].shape
    local = channels // blocks
    steps = rows // local
    peers = max(blocks // 2 - 1, 1)
    return pl.pallas_call(
        functools.partial(mlp_kernel, blocks, count),
        out_shape=[
            jax.ShapeDtypeStruct((blocks, rows, width), BF),
            jax.ShapeDtypeStruct((peers, steps * (2 * local + 16), width), BF),
            jax.ShapeDtypeStruct((2 * rows, width), F32),
            jax.ShapeDtypeStruct((2 * rows, width), F32),
            jax.ShapeDtypeStruct((steps, 1, width), F32),
            jax.ShapeDtypeStruct((steps, 2, width), F32),
            *[jax.ShapeDtypeStruct((2, channels, hid), BF)] * 2,
            jax.ShapeDtypeStruct((3, 8, width), F32),
        ],
        in_specs=[SMEM] + [VMEM] * (2 * blocks + 8),
        out_specs=[VMEM] * 9,
        scratch_shapes=[
            pltpu.VMEM((channels, rows // local * width), BF),
            pltpu.VMEM((channels, rows // local * width), BF),
            pltpu.VMEM((2, hid, rows // local * width), BF),
            pltpu.VMEM((2, hid, rows // local * width), BF),
            pltpu.VMEM((channels, width), F32),
            pltpu.VMEM((channels, 128), F32),
            pltpu.VMEM((channels, width), BF),
            pltpu.VMEM((2, hid, 128), F32),
            pltpu.VMEM((channels, 128), F32),
            pltpu.VMEM((channels, 128), F32),
            pltpu.VMEM((2, hid, 128), F32),
        ],
        compiler_params=grant(22),
        cost_estimate=cost(8),
        name="mlp",
    )(me, *conv, *ct, *weights)


def norm_kernel(peers, count, core_ref, *refs):
    dn_ref, stand_ref, inv_ref, vec_ref, vecx_ref, q_ref, small_ref = refs[:7]
    got = refs[7 : 7 + peers]
    (own_ref, send_ref, edge_own_ref, edge_send_ref, sums_ref, buf, gain_ref, fold_ref) = refs[7 + peers :]
    core = core_ref[0] & 1
    steps = inv_ref.shape[0]
    both = dn_ref.shape[0] // steps
    local = both // 2
    channels = both * (peers + 1)
    mine = pl.ds(pl.multiple_of(core * local, 16), local)
    theirs = pl.ds(pl.multiple_of((1 - core) * local, 16), local)
    last = pl.ds(vec_ref.shape[0] - 16, 16)
    gain_ref[mine, :] = column(vector_of(vec_ref[last, :], count)[0])[:local]
    gain_ref[theirs, :] = column(vector_of(vecx_ref[last, :], count)[0])[:local]
    shift_acc = jnp.zeros((both, 128), F32)
    gain_acc = jnp.zeros((both, 128), F32)
    for i in range(steps):
        rows = pl.ds(i * both, both)
        dn = dn_ref[rows, :]
        q = q_ref[i]
        for p in range(peers):
            start = i * (both + 16)
            dn = dn + got[p][0, pl.ds(start, both), :].astype(F32)
            extra = got[p][0, pl.ds(start + both, 16), :].astype(F32)
            q = q + (extra[0:2] + extra[2:4])
        q = q / channels
        stand = stand_ref[rows, :]
        prod = dn * stand
        shift_acc += dn[:, :128] + dn[:, 128:]
        gain_acc += prod[:, :128] + prod[:, 128:]
        buf[i] = inv_ref[i] * (dn * gain_ref[...] - q[0:1] - stand * q[1:2])
    for i in range(steps):
        own_ref[i] = buf[i, mine, :].astype(BF)
        send_ref[pl.ds(i * local, local), :] = buf[i, theirs, :].astype(BF)
    for i in range(3):
        edge_own_ref[i] = buf[i + core, mine, :].astype(BF)
        edge_send_ref[i] = buf[i + core, theirs, :].astype(BF)
    ones = jnp.ones((8, 128), F32)
    fold_ref[0], fold_ref[1] = shift_acc, gain_acc
    line = small_ref[0, pl.ds(0, 1), :]
    for p in range(peers):
        extra = got[p][0, pl.ds(got[p].shape[1] - 16, 16), :].astype(F32)
        line = line + (extra[4:5] + extra[5:6] + extra[6:7])
    low, high = line[:, :local], line[:, local : 2 * local]
    scale_mine = jnp.where(core == 0, low, high)
    scale_theirs = jnp.where(core == 0, high, low)
    for rows, scale, which in ((mine, scale_mine, 1), (theirs, scale_theirs, 2)):
        pair = [
            lax.dot_general(ones, fold_ref[k, rows, :], NT, preferred_element_type=F32, precision=HI)[:1]
            for k in range(2)
        ]
        bias = small_ref[which, pl.ds(0, 4), pl.ds(0, local)]
        sums = jnp.concatenate(pair + [scale, bias, jnp.zeros((1, local), F32)], axis=0)
        if which == 1:
            sums_ref[...] = sums
        else:
            high = sums.astype(BF).astype(F32)
            middle = (sums - high).astype(BF).astype(F32)
            lines = jnp.concatenate([high, middle, sums - high - middle, jnp.zeros((8, local), F32)], axis=0)
            width = send_ref.shape[1]
            lines = jnp.concatenate([lines, jnp.zeros((32, width - local), F32)], axis=1)
            send_ref[pl.ds(steps * local, 32), :] = lines.astype(BF)


def norm_backward(core, count, dn, stand, inv, vector, vector_x, q, small, got):
    steps, _, width = inv.shape
    both = dn.shape[0] // steps
    local = both // 2
    return pl.pallas_call(
        functools.partial(norm_kernel, len(got), count),
        out_shape=[
            jax.ShapeDtypeStruct((steps, local, width), BF),
            jax.ShapeDtypeStruct((steps * local + 32, width), BF),
            jax.ShapeDtypeStruct((3, local, width), BF),
            jax.ShapeDtypeStruct((3, local, width), BF),
            jax.ShapeDtypeStruct((8, local), F32),
        ],
        in_specs=[SMEM] + [VMEM] * (7 + len(got)),
        out_specs=[VMEM] * 5,
        scratch_shapes=[
            pltpu.VMEM((steps, both, width), F32),
            pltpu.VMEM((both, 1), F32),
            pltpu.VMEM((2, both, 128), F32),
        ],
        compiler_params=grant(5),
        cost_estimate=cost(1.3),
        name="norm_backward",
    )(core, dn, stand, inv, vector, vector_x, q, small, *got)


def fill_tile(rows_ref, own_ref, other_ref, core, local):
    half = own_ref.shape[0]
    for part in range(2):
        lanes = slice(part * 128, part * 128 + 128)
        for i in range(half):
            rows_ref[part, pl.ds(pl.multiple_of((core * half + i) * local, 8), local), :] = (
                own_ref[i, :, lanes].astype(F32))
            rows_ref[part, pl.ds(pl.multiple_of(((1 - core) * half + i) * local, 8), local), :] = (
                other_ref[pl.ds(i * local, local), lanes].astype(F32))


def kernel_grad_kernel(core_ref, own_ref, other_ref, image_ref, vector_ref, sums_ref, dkernel_ref, rows_ref,
                       corr_ref, line_ref):
    local, _, width = image_ref.shape
    height = 2 * own_ref.shape[0]
    count = 7 * height
    span = 16 * SLOTS
    fill_tile(rows_ref, own_ref, other_ref, core_ref[0] & 1, local)
    lane = lax.broadcasted_iota(jnp.int32, (count, span), 1) // SLOTS
    inner_slot = lax.broadcasted_iota(jnp.int32, (7, 128), 1) % SLOTS

    def body(g, carry):
        images = image_ref[pl.ds(g * 16, 16)].reshape(span, width)
        corr = jnp.zeros((count, span), F32)
        for first in range(0, 16, 8):
            stacks = []
            for inner in range(first, first + 8):
                a = rows_ref[0, pl.ds(g * 16 + inner, height, stride=local), :]
                b = rows_ref[1, pl.ds(g * 16 + inner, height, stride=local), :]
                stacks += [jnp.concatenate(shift_halves(a, b, 3 - s), axis=1) for s in range(7)]
            stack = jnp.concatenate(stacks, axis=0).astype(BF)
            value = lax.dot_general(stack, images, NT, preferred_element_type=F32)
            for inner in range(8):
                corr = jnp.where(lane == first + inner, value[inner * count : (inner + 1) * count], corr)
        for part in range(2):
            lanes = slice(part * 128, part * 128 + 128)
            corr_ref[part] = corr[:, lanes]
            line = corr_ref[part, pl.ds(0, 7, stride=height), :]
            for h in range(1, height):
                value = corr_ref[part, pl.ds(h, 7, stride=height), :]
                line = line + jnp.where(
                    inner_slot < SLOTS - h, pltpu.roll(value, 128 - h, 1), pltpu.roll(value, SLOTS - h, 1))
            line_ref[part, g, pl.ds(0, 7), :] = line
        return carry

    lax.fori_loop(0, local // 16, body, 0, unroll=3)
    slot = lax.broadcasted_iota(jnp.int32, (7, span), 1) % SLOTS
    total = jnp.zeros(dkernel_ref.shape, F32)
    for g in range(local // 16):
        lines = jnp.concatenate([line_ref[p, g, pl.ds(0, 7), :] for p in range(2)], axis=1)
        spread = [jnp.where(slot == (r - 3) % SLOTS, lines, 0.0) for r in range(7)] + [jnp.zeros((7, span), F32)]
        pick = (lax.broadcasted_iota(jnp.int32, (local, span), 0) - g * 16
                == lax.broadcasted_iota(jnp.int32, (local, span), 1) // SLOTS).astype(F32)
        total = total + lax.dot_general(
            jnp.concatenate(spread, axis=0), pick, NT, preferred_element_type=F32, precision=HI)
    dkernel_ref[...] = total * grad_scale
    lines = other_ref[pl.ds(height // 2 * local, 32), pl.ds(0, local)].astype(F32)
    sums = (sums_ref[...] + (lines[:8] + lines[8:16] + lines[16:24])) * grad_scale
    start = vector_ref.shape[1] - 128
    scale_line = sums[2:3] / vector_ref[:, start : start + local]
    dkernel_ref[pl.ds(49, 7), :] = jnp.concatenate([sums[:2], scale_line, sums[3:7]], axis=0)


def kernel_grad(core, own, other, image16, vector, sums):
    local = image16.shape[0]
    height = 2 * own.shape[0]
    return pl.pallas_call(
        kernel_grad_kernel,
        out_shape=jax.ShapeDtypeStruct((56, local), F32),
        in_specs=[SMEM] + [VMEM] * 5,
        out_specs=VMEM,
        scratch_shapes=[
            pltpu.VMEM((2, height * local, 128), F32),
            pltpu.VMEM((2, 7 * height, 128), F32),
            pltpu.VMEM((2, local // 16, 8, 128), F32),
        ],
        compiler_params=grant(5),
        cost_estimate=cost(4),
        name="kernel_grad",
    )(core, own, other, image16, vector, sums)


def image_grad_kernel(core_ref, own_ref, other_ref, same_ref, cross_ref, ct_ref, taps_ref, out_ref, rows_ref):
    local, height, width = ct_ref.shape
    core = core_ref[0] & 1
    count = 7 * height
    fill_tile(rows_ref, own_ref, other_ref, core, local)
    for part in range(2):
        lanes = slice(part * 128, part * 128 + 128)
        for i in range(3):
            a = pl.multiple_of((height + 5 * core + i) * local, 8)
            b = pl.multiple_of((height + 5 * (1 - core) + i) * local, 8)
            rows_ref[part, pl.ds(a, local), :] = same_ref[i, :, lanes].astype(F32)
            rows_ref[part, pl.ds(b, local), :] = cross_ref[i, :, lanes].astype(F32)
        rows_ref[part, pl.ds((height + 3) * local, 2 * local), :] = jnp.zeros((2 * local, 128), F32)

    def body(g, carry):
        tiles = []
        for u in range(8):
            pair = [rows_ref[p, pl.ds(g * 8 + u, SLOTS, stride=local), :] for p in range(2)]
            tiles.append(jnp.concatenate(pair, axis=1))
        right = jnp.concatenate(tiles, axis=0).astype(BF)
        start = pl.multiple_of(g * 8 * count, 16)
        products = jnp.dot(taps_ref[pl.ds(start, 8 * count), :], right, preferred_element_type=F32)
        for u in range(8):
            ch = g * 8 + u
            left_right = shift_sum(products[u * count : (u + 1) * count], height, -1)
            out_ref[ch] = (ct_ref[ch].astype(F32) + jnp.concatenate(left_right, axis=1)).astype(BF)
        return carry

    lax.fori_loop(0, local // 8, body, 0, unroll=True)


def image_grad(core, own, other, same, cross, ct, taps):
    local, height, width = ct.shape
    return pl.pallas_call(
        image_grad_kernel,
        out_shape=jax.ShapeDtypeStruct((local, height, width), BF),
        in_specs=[SMEM] + [VMEM] * 6,
        out_specs=VMEM,
        scratch_shapes=[pltpu.VMEM((2, SLOTS * local, 128), F32)],
        compiler_params=grant(6),
        cost_estimate=cost(5),
        name="image_grad",
    )(core, own, other, same, cross, ct, taps)


def finish_kernel(blocks, core_ref, image_ref, vector_ref, *refs):
    part_refs = refs[:blocks]
    out_ref, rows_ref, col_ref = refs[blocks:]
    local, height, width = image_ref.shape
    half = height // 2
    core = core_ref[0] & 1
    col_ref[...] = column(vector_ref[...])
    scale = col_ref[pl.ds(vector_ref.shape[1] - 128, local), :]
    for which in range(2):
        place = core if which == 0 else 1 - core
        for i in range(half):
            rows = pl.ds(i * local, local)
            total = part_refs[which][rows, :].astype(F32)
            for k in range(which + 2, blocks, 2):
                total = total + part_refs[k][rows, :].astype(F32)
            total = total * scale
            start = pl.multiple_of((place * half + i) * local, 8)
            for part in range(2):
                rows_ref[part, pl.ds(start, local), :] = total[:, part * 128 : part * 128 + 128]

    def body(g, carry):
        for u in range(8):
            ch = g * 8 + u
            pair = [rows_ref[p, pl.ds(ch, height, stride=local), :] for p in range(2)]
            out_ref[ch] = (image_ref[ch].astype(F32) + jnp.concatenate(pair, axis=1)).astype(BF)
        return carry

    lax.fori_loop(0, local // 8, body, 0, unroll=6)


def finish(core, image, vector, parts):
    local, height, width = image.shape
    return pl.pallas_call(
        functools.partial(finish_kernel, len(parts)),
        out_shape=jax.ShapeDtypeStruct((local, height, width), BF),
        in_specs=[SMEM] + [VMEM] * (2 + len(parts)),
        out_specs=VMEM,
        scratch_shapes=[
            pltpu.VMEM((2, height * local, 128), F32),
            pltpu.VMEM((vector.shape[1], 1), F32),
        ],
        compiler_params=grant(5),
        cost_estimate=cost(2),
        name="finish",
    )(core, image, vector, *parts)


def totals_kernel(sums_ref, sums_got_ref, dkernel_ref, shift_ref, gain_ref, scale_ref, bias_ref):
    sums = sums_ref[...] + sums_got_ref[...]
    dkernel_ref[...] = sums[:49]
    shift_ref[...], gain_ref[...], scale_ref[...] = sums[49:50], sums[50:51], sums[51:52]
    bias = jnp.concatenate([sums[52 + i : 53 + i] for i in range(4)], axis=1)
    lanes = bias_ref.shape[1]
    bias_ref[...] = jnp.concatenate(
        [bias[:, i * lanes : (i + 1) * lanes] for i in range(bias_ref.shape[0])], axis=0)


def totals(sums, sums_got):
    local = sums.shape[1]
    return pl.pallas_call(
        totals_kernel,
        out_shape=[
            jax.ShapeDtypeStruct((49, local), F32),
            *[jax.ShapeDtypeStruct((1, local), F32)] * 3,
            jax.ShapeDtypeStruct((local // 32, 128) if local % 32 == 0 else (1, 4 * local), F32),
        ],
        in_specs=[VMEM, VMEM],
        out_specs=[VMEM] * 5,
        compiler_params=grant(2),
        cost_estimate=cost(0.4),
        name="totals",
    )(sums, sums_got)


def swap(value, axis, size, k):
    return lax.ppermute(value, axis, [(i, i ^ k) for i in range(size)])


def after(value, *gates):
    return lax.optimization_barrier((value, *gates))[0]


def sum_over_space(value, size):
    k = 1
    while 2 * k < size:
        value = value + swap(value, "space", size, k)
        k *= 2
    return value, k


def scatter_over_space(ids, own, got, size):
    if size > 4:
        total = (own.astype(F32) + got.astype(F32)).astype(BF)
        return [lax.psum_scatter(total, "space", scatter_dimension=1, tiled=True)], total
    mine, *others = merge(ids, own, got, size)
    return [mine] + [swap(p, "space", size, k + 1) for k, p in enumerate(others)], mine


def per_device(image, dw_weight, ln_gain, ln_shift, w_in, b_in, w_out, layer_scale, cotangent):
    local, height, width = image.shape
    hid = w_in.shape[1]
    n_chan, n_space = lax.axis_size("chan"), lax.axis_size("space")
    ids = jnp.stack([lax.axis_index("chan"), lax.axis_index("space")]).astype(jnp.int32)

    used = 2 * local + hid + 128
    count = -(-used // width)
    parts = [ln_gain, ln_shift, b_in, jnp.zeros(count * width - used, F32), layer_scale, jnp.zeros(128 - local, F32)]
    packed = jnp.concatenate([v for v in parts if v.size])[None]
    d_mine, d_theirs = pack(ids, cotangent, packed)
    d_all = [d_mine] + [
        swap(d_theirs if k % 2 else d_mine, "chan", n_chan, k) for k in range(1, n_chan)
    ]
    pairs_a = [(s, s ^ 1) for s in range(n_space) if s ^ 1 < n_space]
    pairs_b = [(s, t) for s in range(n_space) for t in [s + 1 if s % 2 else s - 1] if 0 <= t < n_space]
    edge_a, edge_b = edges(ids, after(image, d_mine))
    got_a = lax.ppermute(edge_a, "space", pairs_a)
    got_b = lax.ppermute(edge_b, "space", pairs_b)
    dw_weight, w_in, w_out = lax.optimization_barrier((dw_weight, w_in, w_out, edge_a))[:3]
    w_inx = swap(w_in, "chan", n_chan, 1)
    w_outx = swap(w_out, "chan", n_chan, 1)
    weight = jnp.pad(dw_weight.T, ((0, 15), (0, -local % 128)))
    taps = make_taps(weight, local, height, False)
    taps, d_all = lax.optimization_barrier((taps, d_all))

    mine, theirs, image16 = conv_forward(ids, image, got_a, got_b, taps)
    conv = [mine] + [swap(theirs if k % 2 else mine, "chan", n_chan, k) for k in range(1, n_chan)]
    w_in, w_inx, w_out, w_outx, weight = lax.optimization_barrier((w_in, w_inx, w_out, w_outx, weight, mine))[:5]
    w_int, w_intx, w_outt, w_outtx = turn(w_in, w_inx, w_out, w_outx)
    taps_back = make_taps(weight, local, height, True)
    weights = [w_in, w_inx, w_int, w_intx, w_out, w_outx, w_outt, w_outtx]
    conv[0] = after(conv[0], taps_back)
    branch, dn_send, dn, stand, inv, q, dw, dw_send, small = mlp(ids, conv, d_all, count, weights)

    got = [swap(dn_send[k - 1 : k], "chan", n_chan, 2 * k) for k in range(1, n_chan // 2)]
    dw, gate = scatter_over_space(ids, dw, swap(dw_send, "chan", n_chan, 1), n_space)
    inv = after(inv, gate)

    dconv, dconv_send, edge, edge_send, sums = norm_backward(
        ids, count, dn, stand, inv, d_all[0], d_all[1], q, small, got)
    same_pairs, cross_pairs = [], []
    for s in range(n_space):
        for c in range(n_chan):
            t = s + 1 if c % 2 else s - 1
            if 0 <= t < n_space:
                same_pairs.append((s * n_chan + c, t * n_chan + c))
                cross_pairs.append((s * n_chan + c, t * n_chan + (c ^ 1)))
    same = lax.ppermute(edge, ("space", "chan"), same_pairs)
    cross = lax.ppermute(edge_send, ("space", "chan"), cross_pairs)
    other = swap(dconv_send, "chan", n_chan, 1)
    dw = sum(term.astype(F32) for term in dw) * grad_scale
    branch = after(branch, other)
    parts = [branch[0]] + [swap(branch[k], "chan", n_chan, k) for k in range(1, n_chan)]

    sums = kernel_grad(ids, dconv, other, image16, packed, after(sums, parts[1]))
    sums, last = sum_over_space(sums, n_space)
    d_image = image_grad(ids, dconv, other, same, cross, cotangent, taps_back)
    sums = after(sums, d_image)
    sums_got = swap(sums, "space", n_space, last)
    output = finish(ids, image, packed, parts)
    d_kernel, d_shift, d_gain, d_scale, d_b_in = totals(sums, sums_got)
    flat = [v.reshape(-1) for v in (d_gain, d_shift, d_b_in, d_scale)]
    return (output, d_image, d_kernel.T, *flat[:2], dw[0], flat[2], dw[1].T, flat[3])


def solution(mesh):
    return jax.shard_map(
        per_device,
        mesh=mesh,
        in_specs=(
            P("chan", ("groups", "space"), None),
            P("chan", None),
            P("chan"),
            P("chan"),
            P(None, "chan"),
            P("chan"),
            P("chan", None),
            P("chan"),
            P("chan", ("groups", "space"), None),
        ),
        out_specs=(
            P("chan", ("groups", "space"), None),
            P("chan", ("groups", "space"), None),
            P("chan", "groups"),
            P(("groups", "chan")),
            P(("groups", "chan")),
            P("space", ("groups", "chan")),
            P(("groups", "chan")),
            P(("groups", "chan"), "space"),
            P(("groups", "chan")),
        ),
        check_vma=False,
    )
```
